128 devices in a mesh: row: 16 (over z_lo, x, core), col: 8 (over y, z_hi).
Axes of the slice: x: 4, y: 4, z: 4 (z_hi: 2, z_lo: 2; z = z_hi * 2 + z_lo), core: 2. Of those that a mesh axis runs over, the one named last changes fastest.
Arguments:
- images: bfloat16 [4, 8, 16, 3072], P(None, 'col', 'row'), may hold values from -6 to 6
- cotangent: bfloat16 [32, 16, 4, 8, 16], P('row', None, None, 'col'), may hold values from -192 to 192
Outputs:
- kernel: float32 [32, 16, 4, 8, 16], P('row', None, None, 'col')
- image_grads: float32 [4, 8, 16, 3072], P(None, 'col', 'row')
The draws below stay inside these ranges and needn't reach their ends.
All inputs are finite; a program needn't handle non-finite values.
Results may differ from the reference program's by a relative error of at most 0.0003.
Values may be sent and summed in bfloat16 or wider, within the bound.
A program may use at most 64 MiB of HBM per device.

```python
import math
import jax
import jax.numpy as jnp
import numpy as np
from jax import lax

CHAN = 3
TILE = 16
LAYERS = 3
FEAT = 3072
NBLK = 32
KB = 4
N_ROW = 16
N_COL = 8


def block_levels(own_key, shape, pieces, smallest, high):
    def one(dim, blocks):
        heights = jax.random.uniform(jax.random.fold_in(jax.random.fold_in(own_key, 6), dim), (blocks,), jnp.float32, smallest / len(pieces), high / len(pieces))
        return jnp.repeat(jnp.exp(heights), shape[dim] // blocks).reshape((-1,) + (1,) * (len(shape) - dim - 1))

    level = one(*pieces[0])
    for cut in pieces[1:]:
        level = level * one(*cut)
    return level


def scatter_about(rng, dims, spread, limit, split=(), kind=jnp.bfloat16):
    values = spread * jax.random.normal(rng, dims, jnp.float32)
    if split:
        values = values * block_levels(rng, dims, split, -0.22, 0.18)
    return jnp.clip(values, -limit, limit).astype(kind)


def setup_inputs(seed: int = 0) -> dict:
    splits = jax.random.split(jax.random.key(seed), 3)
    images = scatter_about(splits[0], (KB, N_COL, TILE, FEAT), 1.0, 6.0, ((1, 8), (2, 16)))
    cotangent = scatter_about(splits[1], (NBLK, TILE, KB, N_COL, TILE), 32.0, 192.0, ((0, 16), (3, 8)))
    return {"images": images, "cotangent": cotangent}


WEIGHT_VAR = 2.0
BIAS_VAR = 0.1

def shifted(field, offset):
    total = field.shape[-1]
    widths = [(0, 0)] * (field.ndim - 1) + [(max(-offset, 0), max(offset, 0))]
    padded = jnp.pad(field, widths)
    begin = max(offset, 0)
    return padded[..., begin:begin + total]

def spatial_blur(field, grid_side):
    column = jnp.arange(grid_side * grid_side) % grid_side
    left_ok = (column > 0).astype(jnp.float32)
    right_ok = (column < grid_side - 1).astype(jnp.float32)
    across = field + shifted(field, -1) * left_ok + shifted(field, 1) * right_ok
    summed = across + shifted(across, -grid_side) + shifted(across, grid_side)
    return WEIGHT_VAR * summed / 9.0 + BIAS_VAR

def relu_expect(cross_cov, left_var, right_var):
    fixed_cross = lax.stop_gradient(cross_cov)
    fixed_left = lax.stop_gradient(left_var)
    fixed_right = lax.stop_gradient(right_var)
    root_prod = jnp.sqrt(fixed_left * fixed_right)
    cosine = jnp.clip(fixed_cross / root_prod, -1.0, 1.0)
    angle_val = jnp.arccos(cosine)
    sine_val = jnp.sqrt(jnp.maximum(1.0 - cosine * cosine, 0.0))
    value = root_prod * (sine_val + (jnp.pi - angle_val) * cosine) / (2.0 * jnp.pi)
    slope_cross = (jnp.pi - angle_val) / (2.0 * jnp.pi)
    slope_left = jnp.sqrt(fixed_right / fixed_left) * sine_val / (4.0 * jnp.pi)
    slope_right = jnp.sqrt(fixed_left / fixed_right) * sine_val / (4.0 * jnp.pi)
    linear = slope_cross * cross_cov + slope_left * left_var + slope_right * right_var
    return lax.stop_gradient(value - linear) + linear

def tile_kernel(left_imgs, right_imgs):
    tile_rows = left_imgs.shape[0]
    positions = left_imgs.shape[1] // CHAN
    grid_side = math.isqrt(positions)
    left_px = left_imgs.reshape(tile_rows, CHAN, positions)
    right_px = right_imgs.reshape(right_imgs.shape[0], CHAN, positions)
    cross_cov = jnp.einsum('acp,bcp->abp', left_px, right_px, precision=lax.Precision.HIGHEST) / CHAN
    left_var = lax.optimization_barrier(jnp.sum(left_px * left_px, axis=1)) / CHAN
    right_var = lax.optimization_barrier(jnp.sum(right_px * right_px, axis=1)) / CHAN
    for layer_idx in range(LAYERS):
        cross_cov = spatial_blur(cross_cov, grid_side)
        left_var = spatial_blur(left_var, grid_side)
        right_var = spatial_blur(right_var, grid_side)
        cross_cov = relu_expect(cross_cov, left_var[:, None, :], right_var[None, :, :])
        left_var = 0.5 * left_var
        right_var = 0.5 * right_var
    return WEIGHT_VAR * lax.optimization_barrier(jnp.mean(cross_cov, axis=-1)) + BIAS_VAR

def tile_terms(left_blk, right_blk, cot_blk):
    left_full = left_blk.astype(jnp.float32)
    right_full = right_blk.astype(jnp.float32)
    value, pullback = jax.vjp(tile_kernel, left_full, right_full)
    grad_left, grad_right = pullback(cot_blk.astype(jnp.float32))
    return (value, grad_left, grad_right)

def reference(images, cotangent):
    block_count = 2 * N_ROW
    blocks = images.reshape(block_count, TILE, FEAT)
    cot_grid = cotangent.reshape(block_count, TILE, block_count, TILE)
    table = np.array([(first, second) for first in range(block_count) for second in range(first, block_count)], dtype=np.int32)
    zero_idx = jnp.zeros((), jnp.int32)

    def step_fn(carry, pair_ids):
        grads, kernel = carry
        first = pair_ids[0].astype(jnp.int32)
        second = pair_ids[1].astype(jnp.int32)
        left_blk = lax.dynamic_index_in_dim(blocks, first, 0, keepdims=False)
        right_blk = lax.dynamic_index_in_dim(blocks, second, 0, keepdims=False)
        cot_blk = lax.dynamic_slice(cot_grid, (first, zero_idx, second, zero_idx), (1, TILE, 1, TILE)).reshape(TILE, TILE)
        value, grad_left, grad_right = tile_terms(left_blk, right_blk, cot_blk)
        grads = grads.at[first].add(grad_left)
        grads = grads.at[second].add(grad_right)
        kernel = lax.dynamic_update_slice(kernel, value.reshape(1, TILE, 1, TILE), (first, zero_idx, second, zero_idx))
        return ((grads, kernel), None)
    start = (jnp.zeros((block_count, TILE, FEAT), jnp.float32), jnp.zeros((block_count, TILE, block_count, TILE), jnp.float32))
    (grads, kernel), unused = lax.scan(step_fn, start, jnp.asarray(table))
    return (kernel.reshape(block_count, TILE, KB, N_COL, TILE), grads.reshape(KB, N_COL, TILE, FEAT))
```

```python
import math

import jax
import jax.numpy as jnp
from jax import lax
from jax.experimental import pallas as pl
from jax.experimental.pallas import tpu as pltpu
from jax.sharding import PartitionSpec as P

WEIGHT_VAR = 2.0
BIAS_VAR = 0.1
LAYERS = 3
ALPHA = [WEIGHT_VAR / 27.0]
for _ in range(LAYERS - 1):
    ALPHA.append(ALPHA[-1] * WEIGHT_VAR / 9.0)
BIAS = [BIAS_VAR / a for a in ALPHA]
ACOS = (
    1.5707957734815379,
    -0.9999221189563077,
    0.7835891615481994,
    -0.6503504235048135,
    0.5139260440580442,
    -0.3310160748218498,
    0.14106763470126799,
    -0.028090549822004016,
)
ASIN = [a / (2.0 * math.pi) for a in ACOS]
TINY = 1e-30
BATCH = 8


def lane_masks(shape):
    lane = lax.broadcasted_iota(jnp.int32, shape, len(shape) - 1)
    f = jnp.float32
    return (
        (lane % 32 != 0).astype(f),
        (lane % 32 != 31).astype(f),
        (lane >= 32).astype(f),
        (lane < 96).astype(f),
    )


def compute_kernel(n_own, n_slots, n_tiles, plan, img, cot, kout, grad, xa, ra, ta, xb, rb, tb, ub, uacc, ua, sg, sz):
    f32 = jnp.float32
    slot_count, bounds, tile_of = plan()
    left, right, upper, lower = lane_masks((16, 128))

    row3 = lax.broadcasted_iota(jnp.int32, (BATCH, 8, 128), 1)
    masks3 = lane_masks((BATCH, 8, 128))

    def image_blur(v):
        across = v + masks3[0] * pltpu.roll(v, 1, 2) + masks3[1] * pltpu.roll(v, 127, 2)
        above = pltpu.roll(across, 1, 1)
        below = pltpu.roll(across, 7, 1)
        above = jnp.where(row3 == 0, masks3[2] * pltpu.roll(above, 32, 2), above)
        below = jnp.where(row3 == 7, masks3[3] * pltpu.roll(below, 96, 2), below)
        return across + above + below

    def prologue(step, carry):
        at = pl.multiple_of(step * BATCH, BATCH)
        at8 = pl.multiple_of(step * BATCH * 8, BATCH * 8)
        val = img[pl.ds(at, BATCH)].astype(f32)
        var = jnp.zeros((BATCH, 8, 128), f32)
        for ch in range(3):
            x = val[:, ch * 8 : ch * 8 + 8, :]
            xa[ch, pl.ds(at8, BATCH * 8), :] = x.reshape(BATCH * 8, 128)
            var = var + x * x
        var = var * (1.0 / 3.0)
        for layer in range(LAYERS):
            area = (WEIGHT_VAR / 9.0) * image_blur(var) + BIAS_VAR
            inv = lax.rsqrt(area)
            ra[layer, pl.ds(at8, BATCH * 8), :] = (inv * math.sqrt(ALPHA[layer])).reshape(BATCH * 8, 128)
            ta[layer, pl.ds(at8, BATCH * 8), :] = (
                area * inv * (1.0 / math.sqrt(2.0 * math.pi * ALPHA[layer]))
            ).reshape(BATCH * 8, 128)
            var = 0.5 * area
        return carry

    batches = (n_own + slot_count + BATCH - 1) // BATCH
    lax.fori_loop(0, batches, prologue, 0)

    for group in range(n_own // 8):
        for s in range(8):
            rows = pl.ds(group * 64 + s, 8, stride=8)
            for q in range(3):
                xb[q, s, group * 8 : group * 8 + 8, :] = xa[q, rows, :]
                rb[q, s, group * 8 : group * 8 + 8, :] = ra[q, rows, :]
                tb[q, s, group * 8 : group * 8 + 8, :] = ta[q, rows, :]
    ub[...] = jnp.zeros_like(ub)
    kout[...] = jnp.zeros_like(kout)

    def across(v):
        return v + left * pltpu.roll(v, 1, 1) + right * pltpu.roll(v, 127, 1)

    def vertical(h, bias):
        top = upper * pltpu.roll(h[7], 32, 1)
        bottom = lower * pltpu.roll(h[0], 96, 1)
        if bias is not None:
            top = top + bias
            bottom = bottom + bias
        w = [None] * 8
        w[0] = (h[0] + h[1]) + top
        w[7] = (h[6] + h[7]) + bottom
        for p in (1, 3, 5):
            mid = h[p] + h[p + 1]
            if bias is not None:
                mid = mid + bias
            w[p] = h[p - 1] + mid
            w[p + 1] = mid + h[p + 2]
        return w

    lane16 = lax.broadcasted_iota(jnp.int32, (16, 128), 1)

    def slot_step(slot, carry):
        low, high = bounds(slot)
        base = (n_own + slot) * 8
        uacc[...] = jnp.zeros_like(uacc)

        def unit(bb, inner):
            own = pl.ds(pl.multiple_of(bb * 16, 16), 16)
            tile, lane = tile_of(slot, bb)

            def arow(ref, q, s):
                return ref[q, pl.ds(base + s, 1), :]

            h = []
            for s in range(8):
                x = xb[0, s, own, :] * arow(xa, 0, s)
                x = x + xb[1, s, own, :] * arow(xa, 1, s)
                x = x + xb[2, s, own, :] * arow(xa, 2, s)
                h.append(across(x))
            weight = jnp.where(lane16 == lane, cot[tile].astype(f32), 0.0)
            weight = jnp.sum(weight, axis=1, keepdims=True) * (WEIGHT_VAR * ALPHA[2] / 1024.0)
            weight = jnp.broadcast_to(weight, (16, 128))
            total = None
            for layer in range(LAYERS):
                w = vertical(h, BIAS[layer])
                h = []
                for s in range(8):
                    c = (w[s] * rb[layer, s, own, :]) * arow(ra, layer, s)
                    y = jnp.maximum(1.0 - c * c, TINY)
                    sine = y * lax.rsqrt(y)
                    poly = ASIN[7] * sine + ASIN[6]
                    for k in range(5, -1, -1):
                        poly = poly * sine + ASIN[k]
                    g = c * poly + 0.25
                    z = (sine * tb[layer, s, own, :]) * arow(ta, layer, s)
                    f = w[s] * g + z
                    if layer < LAYERS - 1:
                        sg[layer, s] = g
                        sz[layer, s] = z
                        h.append(across(f))
                    else:
                        total = f if total is None else total + f
                        e = weight * z
                        ub[layer, s, own, :] += e
                        uacc[layer, s] += e[:8] + e[8:]
                        h.append(across(weight * g))
            value = jnp.sum(total, axis=1, keepdims=True) * (WEIGHT_VAR * ALPHA[2] / 1024.0) + BIAS_VAR
            kout[tile] = jnp.where(lane16 == lane, value, kout[tile])
            for layer in range(LAYERS - 2, -1, -1):
                w = vertical(h, None)
                h = []
                for s in range(8):
                    e = w[s] * sz[layer, s]
                    ub[layer, s, own, :] += e
                    uacc[layer, s] += e[:8] + e[8:]
                    h.append(across(w[s] * sg[layer, s]))
            w = vertical(h, None)
            for s in range(8):
                for q in range(3):
                    ub[3 + q, s, own, :] += w[s] * arow(xa, q, s)
                    e = w[s] * xb[q, s, own, :]
                    uacc[3 + q, s] += e[:8] + e[8:]
            return inner

        lax.fori_loop(low, high, unit, 0)
        for k in range(6):
            for s in range(8):
                ua[k, pl.ds(base + s, 1), :] = jnp.sum(uacc[k, s], axis=0, keepdims=True)
        return carry

    lax.fori_loop(0, slot_count, slot_step, 0)

    for group in range(n_own // 8):
        for s in range(8):
            rows = pl.ds(group * 64 + s, 8, stride=8)
            for k in range(6):
                ua[k, rows, :] = ub[k, s, group * 8 : group * 8 + 8, :]

    def epilogue(step, carry):
        at = pl.multiple_of(step * BATCH, BATCH)
        at8 = pl.ds(pl.multiple_of(step * BATCH * 8, BATCH * 8), BATCH * 8)
        down = None
        for layer in range(LAYERS - 1, -1, -1):
            r = ra[layer, at8, :]
            d = ua[layer, at8, :] * (r * r) * (0.5 / ALPHA[layer])
            d = d.reshape(BATCH, 8, 128)
            if down is not None:
                d = d + 0.5 * down
            down = (WEIGHT_VAR / 9.0) * image_blur(d)
        down = down * (2.0 / 3.0)
        for q in range(3):
            x = xa[q, at8, :].reshape(BATCH, 8, 128)
            part = ua[3 + q, at8, :].reshape(BATCH, 8, 128)
            grad[pl.ds(at, BATCH), q * 8 : q * 8 + 8, :] = part + down * x
        return carry

    lax.fori_loop(0, batches, epilogue, 0)


def compute_call(n_own, n_slots, n_tiles, plan, img, cot):
    total = img.shape[0]
    vm = lambda *shape: pltpu.VMEM(shape, jnp.float32)
    whole = pl.BlockSpec(memory_space=pltpu.VMEM)

    def kernel(*refs):
        compute_kernel(n_own, n_slots, n_tiles, plan, *refs)

    return pl.pallas_call(
        kernel,
        out_shape=(
            jax.ShapeDtypeStruct((n_tiles, 16, 128), jnp.float32),
            jax.ShapeDtypeStruct((total, 24, 128), jnp.float32),
        ),
        in_specs=[whole, whole],
        out_specs=(whole, whole),
        scratch_shapes=[
            vm(3, total * 8, 128),
            vm(3, total * 8, 128),
            vm(3, total * 8, 128),
            vm(3, 8, n_own, 128),
            vm(3, 8, n_own, 128),
            vm(3, 8, n_own, 128),
            vm(6, 8, n_own, 128),
            vm(6, 8, 8, 128),
            vm(6, total * 8, 128),
            vm(2, 8, 16, 128),
            vm(2, 8, 16, 128),
        ],
        compiler_params=pltpu.CompilerParams(vmem_limit_bytes=56 * 1024 * 1024),
    )(img, cot)


def to_rows(images):
    count = images.shape[0]
    return images.reshape(count, 3, 4, 8, 32).transpose(0, 1, 3, 2, 4).reshape(count, 24, 128)


def from_rows(rows):
    count = rows.shape[0]
    return rows.reshape(count, 3, 8, 4, 32).transpose(0, 1, 3, 2, 4).reshape(count, 3072)


ROWS = 16
COLS = 8
EXTRA = 18
SLOTS = 32 + EXTRA
TABLE = 88
TILES = 6
MESH = pl.DeviceIdType.MESH


def place():
    return lax.axis_index("row"), lax.axis_index("col")


def enter(r, c):
    barrier = pltpu.get_barrier_semaphore()

    def greet(i, carry):
        rr, cc = i // COLS, i % COLS

        @pl.when(jnp.logical_or(rr != r, cc != c))
        def _():
            pl.semaphore_signal(barrier, inc=1, device_id=(rr, cc), device_id_type=MESH)

        return carry

    lax.fori_loop(0, ROWS * COLS, greet, 0)
    pl.semaphore_wait(barrier, ROWS * COLS - 1)


def send(r, c, rr, cc, src, dst, send_sem, recv_sem):
    away = jnp.logical_or(rr != r, cc != c)

    @pl.when(away)
    def _():
        pltpu.make_async_remote_copy(src, dst, send_sem, recv_sem, device_id=(rr, cc), device_id_type=MESH).start()

    @pl.when(jnp.logical_not(away))
    def _():
        pltpu.make_async_copy(src, dst, recv_sem).start()


def sent(r, c, rr, cc, src, dst, send_sem, recv_sem):
    @pl.when(jnp.logical_or(rr != r, cc != c))
    def _():
        pltpu.make_async_remote_copy(src, dst, send_sem, recv_sem, device_id=(rr, cc), device_id_type=MESH).wait_send()


def arrived(dst, recv_sem):
    pltpu.make_async_copy(dst, dst, recv_sem).wait()


def image_route(r, c, idx):
    k, m = idx // 17, idx % 17
    block = 4 * k + c // 2
    e = (c % 2) * 16 + r
    d = m % 8
    first = e < 16
    extra = m == 16
    rr = jnp.where(m < 8, block, jnp.where(extra, block + 8, block + 16 - d) % 16)
    cc = jnp.where(extra, jnp.where(first, e // 2, 0), d)
    slot = jnp.where(m < 8, e, jnp.where(extra, 64 + jnp.where(first, e % 2, e - 14), 32 + e))
    return k, rr, cc, slot


def slot_count_of(c):
    return jnp.where(c == 0, 32 + EXTRA, 34)


def cot_route(r, c, h, k):
    block, q = 4 * k + c // 2, c % 2
    dd = block - r
    straight = jnp.logical_or(dd < 8, jnp.logical_and(dd == 8, h == q))
    single = jnp.logical_and(dd >= 0, dd != 8)
    single = jnp.logical_and(single, jnp.logical_or(dd != 0, h <= q))
    rr = jnp.where(dd < 8, r, jnp.where(dd > 8, block, jnp.where(h == q, r, r + 8)))
    cc = jnp.where(dd < 8, dd, 16 - dd)
    slot = jnp.where(dd < 8, h * 2 + q, q * 2 + h)
    return dd, single, straight, rr, cc, slot


def gather_kernel(mine, cots, table, tiles, img_send, img_recv, cot_send, cot_recv, far_send):
    r, c = place()
    enter(r, c)

    def images(op):
        def step(idx, carry):
            k, rr, cc, slot = image_route(r, c, idx)
            op(r, c, rr, cc, mine.at[k], table.at[slot], img_send.at[idx], img_recv.at[slot])
            return carry

        lax.fori_loop(0, 68, step, 0)

    def tangents(op):
        def step(idx, carry):
            h, k = idx // 4, idx % 4
            dd, single, straight, rr, cc, slot = cot_route(r, c, h, k)
            turned = jnp.where(straight, 0, 8)
            src = cots.at[turned + idx]

            @pl.when(single)
            def _():
                op(r, c, rr, cc, src, tiles.at[slot], cot_send.at[idx], cot_recv.at[slot])

            @pl.when(dd == 8)
            def _():
                def far(d, inner):
                    @pl.when(jnp.logical_or(h == 0, d == 0))
                    def _():
                        op(r, c, rr, d, src, tiles.at[4 + h], far_send.at[h * 8 + d], cot_recv.at[4 + h])

                    return inner

                lax.fori_loop(0, COLS, far, 0)

            return carry

        lax.fori_loop(0, 8, step, 0)

    images(send)
    tangents(send)

    def landed(slot, carry):
        arrived(table.at[slot], img_recv.at[slot])
        return carry

    lax.fori_loop(0, 32 + slot_count_of(c), landed, 0)
    for slot in range(TILES):
        needed = (None, None, c != 0, None, None, c == 0)[slot]
        if needed is None:
            arrived(tiles.at[slot], cot_recv.at[slot])
        else:

            @pl.when(needed)
            def _():
                arrived(tiles.at[slot], cot_recv.at[slot])

    images(sent)
    tangents(sent)


def gather_call(mine, cots):
    anyspace = pl.BlockSpec(memory_space=pltpu.VMEM)
    dma = pltpu.SemaphoreType.DMA
    return pl.pallas_call(
        gather_kernel,
        out_shape=(
            jax.ShapeDtypeStruct((TABLE, 24, 128), jnp.bfloat16),
            jax.ShapeDtypeStruct((TILES, 16, 128), jnp.bfloat16),
        ),
        in_specs=[anyspace, anyspace],
        out_specs=(anyspace, anyspace),
        scratch_shapes=[dma((68,)), dma((32 + SLOTS,)), dma((8,)), dma((TILES,)), dma((16,))],
        compiler_params=pltpu.CompilerParams(collective_id=0, has_side_effects=True),
    )(mine, cots)


def partial_route(r, c, slot):
    own = slot < 32
    main = slot < 64
    n = slot - 64
    e = jnp.where(main, slot % 32, jnp.where(n < 2, 2 * c + n, 14 + n))
    block = jnp.where(own, r, jnp.where(main, r + c, r + 8) % 16)
    j = 2 * block + e // 16
    source = jnp.where(own, c, jnp.where(main, 8 + c, 16))
    return e % 16, j % 8, j // 8, source


def tile_route(r, c, slot):
    far = slot >= 4
    bb, qa = slot // 2, slot % 2
    other = jnp.where(far, (r + 8) % 16, (r + c) % 16)
    bb = jnp.where(far, jnp.where(r < 8, qa, 1 - qa), bb)
    ahead = other >= r
    i = jnp.where(ahead, 2 * r + bb, 2 * other + qa)
    j = jnp.where(ahead, 2 * other + qa, 2 * r + bb)
    return i // 2, j % 8, i % 2, j // 8


def reduce_kernel(grads, kouts, image_out, kernel_out, parts, far, part_send, part_recv, tile_send, tile_recv, far_recv):
    r, c = place()
    enter(r, c)

    def partials(op):
        def step(slot, carry):
            rr, cc, k, source = partial_route(r, c, slot)
            op(r, c, rr, cc, grads.at[slot], parts.at[k, source], part_send.at[slot], part_recv.at[k, source])
            return carry

        lax.fori_loop(0, 32 + slot_count_of(c), step, 0)

    def outputs(op):
        for slot in range(TILES):
            rr, cc, h, k = tile_route(r, c, jnp.int32(slot))
            needed = (None, None, c != 0, None, None, c == 0)[slot]
            if slot == 4:
                dst, sem = far.at[c], far_recv.at[c]
            else:
                dst, sem = kernel_out.at[h * 4 + k], tile_recv.at[h * 4 + k]
            if needed is None:
                op(r, c, rr, cc, kouts.at[slot], dst, tile_send.at[slot], sem)
            else:

                @pl.when(needed)
                def _():
                    op(r, c, rr, cc, kouts.at[slot], dst, tile_send.at[slot], sem)

    partials(send)
    outputs(send)

    for h in range(2):
        for k in range(4):
            dd, single, straight, rr, cc, slot = cot_route(r, c, h, k)
            place_ = h * 4 + k
            if h == 0:

                @pl.when(dd == 8)
                def _():
                    for d in range(COLS):
                        arrived(far.at[d], far_recv.at[d])
                    total = far[0]
                    for d in range(1, COLS):
                        total = total + far[d]
                    kernel_out[place_] = total

                get = single
            else:
                get = jnp.logical_or(single, dd == 8)

            @pl.when(get)
            def _():
                arrived(kernel_out.at[place_], tile_recv.at[place_])

            @pl.when(jnp.logical_or(dd < 0, jnp.logical_and(dd == 0, h > c % 2)))
            def _():
                kernel_out[place_] = jnp.zeros((16, 128), jnp.float32)

    for k in range(4):

        def landed(source, carry):
            arrived(parts.at[k, source], part_recv.at[k, source])
            return carry

        lax.fori_loop(0, 17, landed, 0)
        total = parts[k, 0]
        for source in range(1, 17):
            total = total + parts[k, source]
        image_out[k] = total

    partials(sent)
    outputs(sent)


def reduce_call(grads, kouts):
    whole = pl.BlockSpec(memory_space=pltpu.VMEM)
    dma = pltpu.SemaphoreType.DMA
    return pl.pallas_call(
        reduce_kernel,
        out_shape=(
            jax.ShapeDtypeStruct((4, 24, 128), jnp.float32),
            jax.ShapeDtypeStruct((8, 16, 128), jnp.float32),
        ),
        in_specs=[whole, whole],
        out_specs=(whole, whole),
        scratch_shapes=[
            pltpu.VMEM((4, 17, 24, 128), jnp.float32),
            pltpu.VMEM((8, 16, 128), jnp.float32),
            dma((32 + SLOTS,)),
            dma((4, 17)),
            dma((TILES,)),
            dma((8,)),
            dma((8,)),
        ],
        compiler_params=pltpu.CompilerParams(collective_id=1, has_side_effects=True),
    )(grads, kouts)


def plan():
    r, c = place()

    def extra(slot):
        n = slot - 32
        e = jnp.where(n < 2, 2 * c + n, 14 + n)
        return e, jnp.where(r < 8, e // 16, 1 - e // 16)

    def bounds(slot):
        e, half = extra(slot)
        main = slot < 32
        short = jnp.logical_and(c == 0, slot < 16)
        low = jnp.where(main, 0, half)
        high = jnp.where(main, jnp.where(short, 1, 2), half + 1)
        return low, high

    def tile_of(slot, bb):
        e, half = extra(slot)
        main = slot < 32
        return jnp.where(main, bb * 2 + slot // 16, 4 + e // 16), jnp.where(main, slot, e) % 16

    return slot_count_of(c), bounds, tile_of


def body(images, cotangent):
    r, c = place()
    mine = to_rows(images.reshape(4, 3072))
    cot = cotangent.reshape(2, 16, 4, 16).transpose(0, 2, 1, 3).reshape(8, 16, 16)
    cots = jnp.concatenate([cot, cot.swapaxes(1, 2)])
    cots = jnp.pad(cots, ((0, 0), (0, 0), (0, 112)))
    table, tiles = gather_call(mine, cots)
    kouts, grads = compute_call(32, SLOTS, TILES, plan, table, tiles)
    image_out, kernel_out = reduce_call(grads, kouts)
    out = kernel_out[:, :, :16].reshape(2, 4, 16, 16)
    half = jnp.arange(2)[:, None, None, None]
    k = jnp.arange(4)[None, :, None, None]
    dd = 4 * k + c // 2 - r
    straight = jnp.logical_or(dd < 8, jnp.logical_and(dd == 8, half == c % 2))
    out = jnp.where(straight, out, out.swapaxes(2, 3))
    kernel = out.transpose(0, 2, 1, 3).reshape(2, 16, 4, 1, 16)
    return kernel, from_rows(image_out).reshape(4, 1, 1, 3072)


def solution(mesh):
    return jax.shard_map(
        body,
        mesh=mesh,
        in_specs=(P(None, "col", "row", None), P("row", None, None, "col", None)),
        out_specs=(P("row", None, None, "col", None), P(None, "col", "row", None)),
        check_vma=False,
    )
```

```python
import math

import jax
import jax.numpy as jnp
from jax import lax
from jax.experimental import pallas as pl
from jax.experimental.pallas import tpu as pltpu
from jax.sharding import PartitionSpec as P

WEIGHT_VAR = 2.0
BIAS_VAR = 0.1
LAYERS = 3
ALPHA = [WEIGHT_VAR / 27.0]
for _ in range(LAYERS - 1):
    ALPHA.append(ALPHA[-1] * WEIGHT_VAR / 9.0)
BIAS = [BIAS_VAR / a for a in ALPHA]
ASIN = [
    a / (2.0 * math.pi)
    for a in (
        -0.10520251251688581,
        1.0690300997862225,
        0.9916991797412131,
        -0.4865441702586394,
        0.1018140487237715,
    )
]
TINY = 1e-30
BATCH = 8
HALVES = 2


def lane_masks(shape):
    lane = lax.broadcasted_iota(jnp.int32, shape, len(shape) - 1)
    f = jnp.float32
    return (
        (lane % 16 != 0).astype(f),
        (lane % 16 != 15).astype(f),
        (lane >= 16).astype(f),
        (lane < 112).astype(f),
    )


def compute_kernel(n_own, plan, img, cot, kout, grad, xa, ra, ta, xb, rb, tb, *rest):
    ub, ua, save = rest[:6], rest[6:12], (rest[12:23], rest[23:34])
    f32 = jnp.float32
    unit_count, slot_count, unit_of = plan()
    left, right, upper, lower = lane_masks((16, 128))

    row3 = lax.broadcasted_iota(jnp.int32, (BATCH, 8, 128), 1)
    masks3 = lane_masks((BATCH, 8, 128))

    def image_blur(v):
        even = row3 % 2 == 0
        mate = jnp.where(even, pltpu.roll(v, 7, 1), pltpu.roll(v, 1, 1))
        side = jnp.where(even, masks3[0] * pltpu.roll(mate, 1, 2), masks3[1] * pltpu.roll(mate, 127, 2))
        h = v + mate + side
        above = pltpu.roll(h, 2, 1)
        below = pltpu.roll(h, 6, 1)
        above = jnp.where(row3 < 2, masks3[2] * pltpu.roll(above, 16, 2), above)
        below = jnp.where(row3 >= 6, masks3[3] * pltpu.roll(below, 112, 2), below)
        return h + above + below

    def prologue(step, carry):
        at = pl.multiple_of(step * BATCH, BATCH)
        at8 = pl.ds(pl.multiple_of(step * BATCH * 8, BATCH * 8), BATCH * 8)
        val = img[pl.ds(at, BATCH)].astype(f32)
        var = jnp.zeros((BATCH, 8, 128), f32)
        for ch in range(3):
            x = val[:, ch * 8 : ch * 8 + 8, :]
            xa[ch, at8, :] = x.reshape(BATCH * 8, 128)
            var = var + x * x
        var = var * (1.0 / 3.0)
        for layer in range(LAYERS):
            area = (WEIGHT_VAR / 9.0) * image_blur(var) + BIAS_VAR
            inv = lax.rsqrt(area)
            ra[layer, at8, :] = (inv * math.sqrt(ALPHA[layer])).reshape(BATCH * 8, 128)
            ta[layer, at8, :] = (
                area * inv * (1.0 / math.sqrt(2.0 * math.pi * ALPHA[layer]))
            ).reshape(BATCH * 8, 128)
            var = 0.5 * area
        for k in range(6):
            ua[k][at8, :] = jnp.zeros((BATCH * 8, 128), f32)
        return carry

    batches = (n_own + slot_count + BATCH - 1) // BATCH
    lax.fori_loop(0, batches, prologue, 0)

    for group in range(n_own // 8):
        for s in range(8):
            rows = pl.ds(group * 64 + s, 8, stride=8)
            part = slice(group * 8, group * 8 + 8)
            for q in range(3):
                xb[q, s, part, :] = xa[q, rows, :]
                rb[q, s, part, :] = ra[q, rows, :]
                tb[q, s, part, :] = ta[q, rows, :]
    for k in range(6):
        ub[k][...] = jnp.zeros_like(ub[k])
    kout[...] = jnp.zeros_like(kout)

    def across(v):
        out = [None] * 8
        for p in range(0, 8, 2):
            mid = v[p] + v[p + 1]
            out[p] = mid + left * pltpu.roll(v[p + 1], 1, 1)
            out[p + 1] = mid + right * pltpu.roll(v[p], 127, 1)
        return out

    def vertical(h, bias):
        w = [None] * 8
        for sx in range(2):
            top = upper * pltpu.roll(h[6 + sx], 16, 1)
            bottom = lower * pltpu.roll(h[sx], 112, 1)
            one = h[sx] + h[2 + sx]
            two = h[4 + sx] + h[6 + sx]
            if bias is not None:
                one = one + bias
                two = two + bias
            w[sx] = one + top
            w[2 + sx] = one + h[4 + sx]
            w[4 + sx] = h[2 + sx] + two
            w[6 + sx] = two + bottom
        return w

    lane16 = lax.broadcasted_iota(jnp.int32, (16, 128), 1)
    ORDER = (0, 7, 1, 6, 2, 5, 3, 4)

    def ready(u):
        live = u < unit_count
        slot, bb, tile, lane = unit_of(jnp.minimum(u, unit_count - 1))
        base = pl.multiple_of((n_own + slot) * 8, 8)
        own = pl.ds(pl.multiple_of(bb * 16, 16), 16)
        return live, base, own, tile, lane

    def arow(ref, q, base, s):
        return ref[q, pl.ds(base + s, 1), :]

    def fold(uacc, k, base):
        total = uacc[k][pl.ds(0, 8, stride=8), :]
        for b in range(1, 8):
            total = total + uacc[k][pl.ds(b, 8, stride=8), :]
        ua[k][pl.ds(base, 8), :] += total

    def tally(uacc, k, s, own, e_own, e_slot):
        ub[k][s, own, :] += e_own
        uacc[k][s * 8 : s * 8 + 8, :] = e_slot[:8] + e_slot[8:]

    def forward(u, saved):
        sg1, sz1, sg2, sz2, sh, *uacc = saved
        live, base, own, tile, lane = ready(u)
        h = [None] * 8
        for s in ORDER:
            x = xb[0, s, own, :] * arow(xa, 0, base, s)
            x = x + xb[1, s, own, :] * arow(xa, 1, base, s)
            x = x + xb[2, s, own, :] * arow(xa, 2, base, s)
            h[s] = x
        h = across(h)
        weight = jnp.where(lane16 == lane, cot[tile].astype(f32), 0.0)
        weight = jnp.sum(weight, axis=1, keepdims=True) * (WEIGHT_VAR * ALPHA[2] / 1024.0)
        weight = jnp.where(live, jnp.broadcast_to(weight, (16, 128)), 0.0)
        total = None
        for layer in range(LAYERS):
            w = vertical(h, BIAS[layer])
            h = [None] * 8
            for s in ORDER:
                c = (w[s] * rb[layer, s, own, :]) * arow(ra, layer, base, s)
                y = jnp.maximum(1.0 - c * c, TINY)
                sine = y * lax.rsqrt(y)
                v = lax.rsqrt(1.0 + sine)
                poly = ASIN[4] * v + ASIN[3]
                for k in range(2, -1, -1):
                    poly = poly * v + ASIN[k]
                g = c * poly + 0.25
                z = (sine * tb[layer, s, own, :]) * arow(ta, layer, base, s)
                f = w[s] * g + z
                if layer < LAYERS - 1:
                    (sg1, sg2)[layer][s] = g
                    (sz1, sz2)[layer][s] = z
                    h[s] = f
                else:
                    total = f if total is None else total + f
                    e = weight * z
                    tally(uacc, layer, s, own, e, e)
                    h[s] = weight * g
            h = across(h)
        for s in range(8):
            sh[s] = h[s]
        fold(uacc, LAYERS - 1, base)
        value = jnp.sum(total, axis=1, keepdims=True) * (WEIGHT_VAR * ALPHA[2] / 1024.0) + BIAS_VAR
        kout[tile] = jnp.where(lane16 == lane, value, kout[tile])

    def backward(u, saved):
        sg1, sz1, sg2, sz2, sh, *uacc = saved
        live, base, own, tile, lane = ready(u)
        h = [sh[s] for s in range(8)]
        for layer in range(LAYERS - 2, -1, -1):
            w = vertical(h, None)
            h = [None] * 8
            for s in ORDER:
                e = w[s] * (sz1, sz2)[layer][s]
                tally(uacc, layer, s, own, e, e)
                h[s] = w[s] * (sg1, sg2)[layer][s]
            h = across(h)
            fold(uacc, layer, base)
        w = vertical(h, None)
        for s in range(8):
            for q in range(3):
                tally(uacc, 3 + q, s, own, w[s] * arow(xa, q, base, s), w[s] * xb[q, s, own, :])
        for q in range(3):
            fold(uacc, 3 + q, base)

    forward(jnp.int32(0), save[0])
    forward(jnp.int32(1), save[1])

    def pair(i, carry):
        backward(2 * i, save[0])
        forward(2 * i + 2, save[0])
        backward(2 * i + 1, save[1])
        forward(2 * i + 3, save[1])
        return carry

    lax.fori_loop(0, unit_count // 2, pair, 0)

    for group in range(n_own // 8):
        for s in range(8):
            rows = pl.ds(group * 64 + s, 8, stride=8)
            for k in range(6):
                ua[k][rows, :] = ub[k][s, group * 8 : group * 8 + 8, :]

    def epilogue(step, carry):
        at = pl.multiple_of(step * BATCH, BATCH)
        at8 = pl.ds(pl.multiple_of(step * BATCH * 8, BATCH * 8), BATCH * 8)
        down = None
        for layer in range(LAYERS - 1, -1, -1):
            r = ra[layer, at8, :]
            d = ua[layer][at8, :] * (r * r) * (0.5 / ALPHA[layer])
            d = d.reshape(BATCH, 8, 128)
            if down is not None:
                d = d + 0.5 * down
            down = (WEIGHT_VAR / 9.0) * image_blur(d)
        down = down * (2.0 / 3.0)
        for q in range(3):
            x = xa[q, at8, :].reshape(BATCH, 8, 128)
            part = ua[3 + q][at8, :].reshape(BATCH, 8, 128)
            grad[pl.ds(at, BATCH), q * 8 : q * 8 + 8, :] = part + down * x
        return carry

    lax.fori_loop(0, batches, epilogue, 0)


def compute_call(n_own, n_tiles, plan, img, cot):
    total = img.shape[0]
    vm = lambda *shape: pltpu.VMEM(shape, jnp.float32)
    whole = pl.BlockSpec(memory_space=pltpu.VMEM)

    def kernel(*refs):
        compute_kernel(n_own, plan, *refs)

    return pl.pallas_call(
        kernel,
        out_shape=(
            jax.ShapeDtypeStruct((n_tiles, 16, 128), jnp.float32),
            jax.ShapeDtypeStruct((total, 24, 128), jnp.float32),
        ),
        in_specs=[whole, whole],
        out_specs=(whole, whole),
        scratch_shapes=[vm(3, total * 8, 128)] * 3
        + [vm(3, 8, n_own, 128)] * 3
        + [vm(8, n_own, 128)] * 6
        + [vm(total * 8, 128)] * 6
        + ([vm(8, 16, 128)] * 5 + [vm(64, 128)] * 6) * 2,
        compiler_params=pltpu.CompilerParams(vmem_limit_bytes=56 * 1024 * 1024),
    )(img, cot)


def to_rows(images):
    count = images.shape[0]
    return images.reshape(count, 3, 8, 4, 16, 2).transpose(0, 1, 3, 5, 2, 4).reshape(count, 24, 128)


def from_rows(rows):
    count = rows.shape[0]
    return rows.reshape(count, 3, 4, 2, 8, 16).transpose(0, 1, 4, 2, 5, 3).reshape(count, 3072)


ROWS = 16
COLS = 8
EXTRA = 18
SLOTS = 32 + EXTRA
TABLE = 88
TILES = 6
MESH = pl.DeviceIdType.MESH


def place():
    return lax.axis_index("row"), lax.axis_index("col")


def enter(r, c):
    barrier = pltpu.get_barrier_semaphore()

    def greet(i, carry):
        rr, cc = i // COLS, i % COLS

        @pl.when(jnp.logical_or(rr != r, cc != c))
        def _():
            pl.semaphore_signal(barrier, inc=1, device_id=(rr, cc), device_id_type=MESH)

        return carry

    lax.fori_loop(0, ROWS * COLS, greet, 0)
    pl.semaphore_wait(barrier, ROWS * COLS - 1)


def send(r, c, rr, cc, src, dst, send_sem, recv_sem):
    away = jnp.logical_or(rr != r, cc != c)

    @pl.when(away)
    def _():
        pltpu.make_async_remote_copy(src, dst, send_sem, recv_sem, device_id=(rr, cc), device_id_type=MESH).start()

    @pl.when(jnp.logical_not(away))
    def _():
        pltpu.make_async_copy(src, dst, recv_sem).start()


def sent(r, c, rr, cc, src, dst, send_sem, recv_sem):
    @pl.when(jnp.logical_or(rr != r, cc != c))
    def _():
        pltpu.make_async_remote_copy(src, dst, send_sem, recv_sem, device_id=(rr, cc), device_id_type=MESH).wait_send()


def arrived(dst, recv_sem):
    pltpu.make_async_copy(dst, dst, recv_sem).wait()


def image_route(r, c, idx):
    k, m = idx // 17, idx % 17
    block = 4 * k + c // 2
    e = (c % 2) * 16 + r
    d = m % 8
    first = e < 16
    extra = m == 16
    rr = jnp.where(m < 8, block, jnp.where(extra, block + 8, block + 16 - d) % 16)
    cc = jnp.where(extra, jnp.where(first, e // 2, 0), d)
    slot = jnp.where(m < 8, e, jnp.where(extra, 64 + jnp.where(first, e % 2, e - 14), 32 + e))
    return k, rr, cc, slot


def slot_count_of(c):
    return jnp.where(c == 0, 32 + EXTRA, 34)


def cot_route(r, c, h, k):
    block, q = 4 * k + c // 2, c % 2
    dd = block - r
    straight = jnp.logical_or(dd < 8, jnp.logical_and(dd == 8, h == q))
    single = jnp.logical_and(dd >= 0, dd != 8)
    single = jnp.logical_and(single, jnp.logical_or(dd != 0, h <= q))
    rr = jnp.where(dd < 8, r, jnp.where(dd > 8, block, jnp.where(h == q, r, r + 8)))
    cc = jnp.where(dd < 8, dd, 16 - dd)
    slot = jnp.where(dd < 8, h * 2 + q, q * 2 + h)
    return dd, single, straight, rr, cc, slot


def gather_kernel(mine, cots, table, tiles, img_send, img_recv, cot_send, cot_recv, far_send):
    r, c = place()
    enter(r, c)

    def images(op):
        def step(idx, carry):
            k, rr, cc, slot = image_route(r, c, idx)
            op(r, c, rr, cc, mine.at[k], table.at[slot], img_send.at[idx], img_recv.at[slot])
            return carry

        lax.fori_loop(0, 68, step, 0)

    def tangents(op):
        def step(idx, carry):
            h, k = idx // 4, idx % 4
            dd, single, straight, rr, cc, slot = cot_route(r, c, h, k)
            turned = jnp.where(straight, 0, 8)
            src = cots.at[turned + idx]

            @pl.when(single)
            def _():
                op(r, c, rr, cc, src, tiles.at[slot], cot_send.at[idx], cot_recv.at[slot])

            @pl.when(dd == 8)
            def _():
                def far(d, inner):
                    @pl.when(jnp.logical_or(h == 0, d == 0))
                    def _():
                        op(r, c, rr, d, src, tiles.at[4 + h], far_send.at[h * 8 + d], cot_recv.at[4 + h])

                    return inner

                lax.fori_loop(0, COLS, far, 0)

            return carry

        lax.fori_loop(0, 8, step, 0)

    images(send)
    tangents(send)

    def landed(slot, carry):
        arrived(table.at[slot], img_recv.at[slot])
        return carry

    lax.fori_loop(0, 32 + slot_count_of(c), landed, 0)
    for slot in range(TILES):
        needed = (None, None, c != 0, None, None, c == 0)[slot]
        if needed is None:
            arrived(tiles.at[slot], cot_recv.at[slot])
        else:

            @pl.when(needed)
            def _():
                arrived(tiles.at[slot], cot_recv.at[slot])

    images(sent)
    tangents(sent)


def gather_call(mine, cots):
    anyspace = pl.BlockSpec(memory_space=pltpu.VMEM)
    dma = pltpu.SemaphoreType.DMA
    return pl.pallas_call(
        gather_kernel,
        out_shape=(
            jax.ShapeDtypeStruct((TABLE, 24, 128), jnp.bfloat16),
            jax.ShapeDtypeStruct((TILES, 16, 128), jnp.bfloat16),
        ),
        in_specs=[anyspace, anyspace],
        out_specs=(anyspace, anyspace),
        scratch_shapes=[dma((68,)), dma((32 + SLOTS,)), dma((8,)), dma((TILES,)), dma((16,))],
        compiler_params=pltpu.CompilerParams(collective_id=0, has_side_effects=True),
    )(mine, cots)


def partial_route(r, c, slot):
    own = slot < 32
    main = slot < 64
    n = slot - 64
    e = jnp.where(main, slot % 32, jnp.where(n < 2, 2 * c + n, 14 + n))
    block = jnp.where(own, r, jnp.where(main, r + c, r + 8) % 16)
    j = 2 * block + e // 16
    source = jnp.where(own, c, jnp.where(main, 8 + c, 16))
    return e % 16, j % 8, j // 8, source


def tile_route(r, c, slot):
    far = slot >= 4
    bb, qa = slot // 2, slot % 2
    other = jnp.where(far, (r + 8) % 16, (r + c) % 16)
    bb = jnp.where(far, jnp.where(r < 8, qa, 1 - qa), bb)
    ahead = other >= r
    i = jnp.where(ahead, 2 * r + bb, 2 * other + qa)
    j = jnp.where(ahead, 2 * other + qa, 2 * r + bb)
    return i // 2, j % 8, i % 2, j // 8


def reduce_kernel(grads, kouts, image_out, kernel_out, parts, far, part_send, part_recv, tile_send, tile_recv, far_recv):
    r, c = place()
    enter(r, c)

    def partials(op):
        def step(slot, carry):
            rr, cc, k, source = partial_route(r, c, slot)
            op(r, c, rr, cc, grads.at[slot], parts.at[k, source], part_send.at[slot], part_recv.at[k, source])
            return carry

        lax.fori_loop(0, 32 + slot_count_of(c), step, 0)

    def outputs(op):
        for slot in range(TILES):
            rr, cc, h, k = tile_route(r, c, jnp.int32(slot))
            needed = (None, None, c != 0, None, None, c == 0)[slot]
            if slot == 4:
                dst, sem = far.at[c], far_recv.at[c]
            else:
                dst, sem = kernel_out.at[h * 4 + k], tile_recv.at[h * 4 + k]
            if needed is None:
                op(r, c, rr, cc, kouts.at[slot], dst, tile_send.at[slot], sem)
            else:

                @pl.when(needed)
                def _():
                    op(r, c, rr, cc, kouts.at[slot], dst, tile_send.at[slot], sem)

    partials(send)
    outputs(send)

    for h in range(2):
        for k in range(4):
            dd, single, straight, rr, cc, slot = cot_route(r, c, h, k)
            place_ = h * 4 + k
            if h == 0:

                @pl.when(dd == 8)
                def _():
                    for d in range(COLS):
                        arrived(far.at[d], far_recv.at[d])
                    total = far[0]
                    for d in range(1, COLS):
                        total = total + far[d]
                    kernel_out[place_] = total

                get = single
            else:
                get = jnp.logical_or(single, dd == 8)

            @pl.when(get)
            def _():
                arrived(kernel_out.at[place_], tile_recv.at[place_])

            @pl.when(jnp.logical_or(dd < 0, jnp.logical_and(dd == 0, h > c % 2)))
            def _():
                kernel_out[place_] = jnp.zeros((16, 128), jnp.float32)

    for k in range(4):

        def landed(source, carry):
            arrived(parts.at[k, source], part_recv.at[k, source])
            return carry

        lax.fori_loop(0, 17, landed, 0)
        total = parts[k, 0]
        for source in range(1, 17):
            total = total + parts[k, source]
        image_out[k] = total

    partials(sent)
    outputs(sent)


def reduce_call(grads, kouts):
    whole = pl.BlockSpec(memory_space=pltpu.VMEM)
    dma = pltpu.SemaphoreType.DMA
    return pl.pallas_call(
        reduce_kernel,
        out_shape=(
            jax.ShapeDtypeStruct((4, 24, 128), jnp.float32),
            jax.ShapeDtypeStruct((8, 16, 128), jnp.float32),
        ),
        in_specs=[whole, whole],
        out_specs=(whole, whole),
        scratch_shapes=[
            pltpu.VMEM((4, 17, 24, 128), jnp.float32),
            pltpu.VMEM((8, 16, 128), jnp.float32),
            dma((32 + SLOTS,)),
            dma((4, 17)),
            dma((TILES,)),
            dma((8,)),
            dma((8,)),
        ],
        compiler_params=pltpu.CompilerParams(collective_id=1, has_side_effects=True),
    )(grads, kouts)


def plan():
    r, c = place()

    def unit_of(u):
        first = c == 0
        n = u - jnp.where(first, 48, 64)
        main = n < 0
        e = jnp.where(n < 2, 2 * c + n, 14 + n)
        half = jnp.where(r < 8, e // 16, 1 - e // 16)
        short = jnp.logical_and(first, u < 16)
        v = jnp.where(first, u + 16, u)
        slot = jnp.where(main, jnp.where(short, u, v // 2), 32 + n)
        bb = jnp.where(main, jnp.where(short, 0, v % 2), half)
        tile = jnp.where(main, bb * 2 + slot // 16, 4 + e // 16)
        return slot, bb, tile, jnp.where(main, slot, e) % 16

    return 66, slot_count_of(c), unit_of


def body(images, cotangent):
    r, c = place()
    mine = to_rows(images.reshape(4, 3072))
    cot = cotangent.reshape(2, 16, 4, 16).transpose(0, 2, 1, 3).reshape(8, 16, 16)
    cots = jnp.concatenate([cot, cot.swapaxes(1, 2)])
    cots = jnp.pad(cots, ((0, 0), (0, 0), (0, 112)))
    table, tiles = gather_call(mine, cots)
    kouts, grads = compute_call(32, TILES, plan, table, tiles)
    image_out, kernel_out = reduce_call(grads, kouts)
    out = kernel_out[:, :, :16].reshape(2, 4, 16, 16)
    half = jnp.arange(2)[:, None, None, None]
    k = jnp.arange(4)[None, :, None, None]
    dd = 4 * k + c // 2 - r
    straight = jnp.logical_or(dd < 8, jnp.logical_and(dd == 8, half == c % 2))
    out = jnp.where(straight, out, out.swapaxes(2, 3))
    kernel = out.transpose(0, 2, 1, 3).reshape(2, 16, 4, 1, 16)
    return kernel, from_rows(image_out).reshape(4, 1, 1, 3072)


def solution(mesh):
    return jax.shard_map(
        body,
        mesh=mesh,
        in_specs=(P(None, "col", "row", None), P("row", None, None, "col", None)),
        out_specs=(P("row", None, None, "col", None), P(None, "col", "row", None)),
        check_vma=False,
    )
```

```python
import math

import jax
import jax.numpy as jnp
from jax import lax
from jax.experimental import pallas as pl
from jax.experimental.pallas import tpu as pltpu
from jax.sharding import PartitionSpec as P

WEIGHT_VAR = 2.0
BIAS_VAR = 0.1
LAYERS = 3
ALPHA = [WEIGHT_VAR / 27.0]
for _ in range(LAYERS - 1):
    ALPHA.append(ALPHA[-1] * WEIGHT_VAR / 9.0)
BIAS = [BIAS_VAR / a for a in ALPHA]
ASIN = [
    a / (2.0 * math.pi)
    for a in (
        -0.10520251251688581,
        1.0690300997862225,
        0.9916991797412131,
        -0.4865441702586394,
        0.1018140487237715,
    )
]
TINY = 1e-30
BATCH = 8
HALVES = 2


def lane_masks(shape):
    lane = lax.broadcasted_iota(jnp.int32, shape, len(shape) - 1)
    f = jnp.float32
    return (
        (lane % 16 != 0).astype(f),
        (lane % 16 != 15).astype(f),
        (lane >= 16).astype(f),
        (lane < 112).astype(f),
    )


def compute_kernel(n_own, plan, img, cot, kout, grad, xa, ra, ta, xb, rb, tb, *rest):
    ub, ua, save = rest[:6], rest[6:12], (rest[12:23], rest[23:34])
    f32 = jnp.float32
    unit_count, slot_count, unit_of = plan()
    left, right, upper, lower = lane_masks((16, 128))

    row3 = lax.broadcasted_iota(jnp.int32, (BATCH, 8, 128), 1)
    masks3 = lane_masks((BATCH, 8, 128))

    def image_blur(v):
        even = row3 % 2 == 0
        mate = jnp.where(even, pltpu.roll(v, 7, 1), pltpu.roll(v, 1, 1))
        side = jnp.where(even, masks3[0] * pltpu.roll(mate, 1, 2), masks3[1] * pltpu.roll(mate, 127, 2))
        h = v + mate + side
        above = pltpu.roll(h, 2, 1)
        below = pltpu.roll(h, 6, 1)
        above = jnp.where(row3 < 2, masks3[2] * pltpu.roll(above, 16, 2), above)
        below = jnp.where(row3 >= 6, masks3[3] * pltpu.roll(below, 112, 2), below)
        return h + above + below

    def prologue(step, carry):
        at = pl.multiple_of(step * BATCH, BATCH)
        at8 = pl.ds(pl.multiple_of(step * BATCH * 8, BATCH * 8), BATCH * 8)
        val = img[pl.ds(at, BATCH)].astype(f32)
        var = jnp.zeros((BATCH, 8, 128), f32)
        for ch in range(3):
            x = val[:, ch * 8 : ch * 8 + 8, :]
            xa[ch, at8, :] = x.reshape(BATCH * 8, 128)
            var = var + x * x
        var = var * (1.0 / 3.0)
        for layer in range(LAYERS):
            area = (WEIGHT_VAR / 9.0) * image_blur(var) + BIAS_VAR
            inv = lax.rsqrt(area)
            ra[layer, at8, :] = (inv * math.sqrt(ALPHA[layer])).reshape(BATCH * 8, 128)
            ta[layer, at8, :] = (
                area * inv * (1.0 / math.sqrt(2.0 * math.pi * ALPHA[layer]))
            ).reshape(BATCH * 8, 128)
            var = 0.5 * area
        for k in range(6):
            ua[k][at8, :] = jnp.zeros((BATCH * 8, 128), f32)
        return carry

    batches = (n_own + slot_count + BATCH - 1) // BATCH
    lax.fori_loop(0, batches, prologue, 0)

    for group in range(n_own // 8):
        for s in range(8):
            rows = pl.ds(group * 64 + s, 8, stride=8)
            part = slice(group * 8, group * 8 + 8)
            for q in range(3):
                xb[q, s, part, :] = xa[q, rows, :]
                rb[q, s, part, :] = ra[q, rows, :]
                tb[q, s, part, :] = ta[q, rows, :]
    for k in range(6):
        ub[k][...] = jnp.zeros_like(ub[k])
    kout[...] = jnp.zeros_like(kout)

    def across(v):
        out = [None] * 8
        for p in range(0, 8, 2):
            mid = v[p] + v[p + 1]
            out[p] = mid + left * pltpu.roll(v[p + 1], 1, 1)
            out[p + 1] = mid + right * pltpu.roll(v[p], 127, 1)
        return out

    def vertical(h, bias):
        w = [None] * 8
        for sx in range(2):
            top = upper * pltpu.roll(h[6 + sx], 16, 1)
            bottom = lower * pltpu.roll(h[sx], 112, 1)
            one = h[sx] + h[2 + sx]
            two = h[4 + sx] + h[6 + sx]
            if bias is not None:
                one = one + bias
                two = two + bias
            w[sx] = one + top
            w[2 + sx] = one + h[4 + sx]
            w[4 + sx] = h[2 + sx] + two
            w[6 + sx] = two + bottom
        return w

    lane16 = lax.broadcasted_iota(jnp.int32, (16, 128), 1)
    ORDER = (0, 7, 1, 6, 2, 5, 3, 4)

    def ready(u):
        live = u < unit_count
        slot, bb, tile, lane = unit_of(jnp.minimum(u, unit_count - 1))
        base = pl.multiple_of((n_own + slot) * 8, 8)
        own = pl.ds(pl.multiple_of(bb * 16, 16), 16)
        return live, base, own, tile, lane

    def arow(ref, q, base, s):
        return ref[q, pl.ds(base + s, 1), :]

    def fold(uacc, k, base):
        total = uacc[k][pl.ds(0, 8, stride=8), :]
        for b in range(1, 8):
            total = total + uacc[k][pl.ds(b, 8, stride=8), :]
        ua[k][pl.ds(base, 8), :] += total

    def tally(uacc, k, s, own, e_own, e_slot):
        ub[k][s, own, :] += e_own
        uacc[k][s * 8 : s * 8 + 8, :] = e_slot[:8] + e_slot[8:]

    def forward(u, saved):
        sg1, sz1, sg2, sz2, sh, *uacc = saved
        live, base, own, tile, lane = ready(u)
        h = [None] * 8
        for s in ORDER:
            x = xb[0, s, own, :] * arow(xa, 0, base, s)
            x = x + xb[1, s, own, :] * arow(xa, 1, base, s)
            x = x + xb[2, s, own, :] * arow(xa, 2, base, s)
            h[s] = x
        h = across(h)
        weight = jnp.where(lane16 == lane, cot[tile].astype(f32), 0.0)
        weight = jnp.sum(weight, axis=1, keepdims=True) * (WEIGHT_VAR * ALPHA[2] / 1024.0)
        weight = jnp.where(live, jnp.broadcast_to(weight, (16, 128)), 0.0)
        total = None
        for layer in range(LAYERS):
            w = vertical(h, BIAS[layer])
            h = [None] * 8
            for s in ORDER:
                c = (w[s] * rb[layer, s, own, :]) * arow(ra, layer, base, s)
                y = jnp.maximum(1.0 - c * c, TINY)
                sine = y * lax.rsqrt(y)
                v = lax.rsqrt(1.0 + sine)
                poly = ASIN[4] * v + ASIN[3]
                for k in range(2, -1, -1):
                    poly = poly * v + ASIN[k]
                g = c * poly + 0.25
                z = (sine * tb[layer, s, own, :]) * arow(ta, layer, base, s)
                f = w[s] * g + z
                if layer < LAYERS - 1:
                    (sg1, sg2)[layer][s] = g
                    (sz1, sz2)[layer][s] = z
                    h[s] = f
                else:
                    total = f if total is None else total + f
                    e = weight * z
                    tally(uacc, layer, s, own, e, e)
                    h[s] = weight * g
            h = across(h)
        for s in range(8):
            sh[s] = h[s]
        fold(uacc, LAYERS - 1, base)
        value = jnp.sum(total, axis=1, keepdims=True) * (WEIGHT_VAR * ALPHA[2] / 1024.0) + BIAS_VAR
        kout[tile] = jnp.where(lane16 == lane, value, kout[tile])

    def backward(u, saved):
        sg1, sz1, sg2, sz2, sh, *uacc = saved
        live, base, own, tile, lane = ready(u)
        h = [sh[s] for s in range(8)]
        for layer in range(LAYERS - 2, -1, -1):
            w = vertical(h, None)
            h = [None] * 8
            for s in ORDER:
                e = w[s] * (sz1, sz2)[layer][s]
                tally(uacc, layer, s, own, e, e)
                h[s] = w[s] * (sg1, sg2)[layer][s]
            h = across(h)
            fold(uacc, layer, base)
        w = vertical(h, None)
        for s in range(8):
            for q in range(3):
                tally(uacc, 3 + q, s, own, w[s] * arow(xa, q, base, s), w[s] * xb[q, s, own, :])
        for q in range(3):
            fold(uacc, 3 + q, base)

    forward(jnp.int32(0), save[0])
    forward(jnp.int32(1), save[1])

    def pair(i, carry):
        backward(2 * i, save[0])
        forward(2 * i + 2, save[0])
        backward(2 * i + 1, save[1])
        forward(2 * i + 3, save[1])
        return carry

    lax.fori_loop(0, unit_count // 2, pair, 0)

    for group in range(n_own // 8):
        for s in range(8):
            rows = pl.ds(group * 64 + s, 8, stride=8)
            for k in range(6):
                ua[k][rows, :] = ub[k][s, group * 8 : group * 8 + 8, :]

    def epilogue(step, carry):
        at = pl.multiple_of(step * BATCH, BATCH)
        at8 = pl.ds(pl.multiple_of(step * BATCH * 8, BATCH * 8), BATCH * 8)
        down = None
        for layer in range(LAYERS - 1, -1, -1):
            r = ra[layer, at8, :]
            d = ua[layer][at8, :] * (r * r) * (0.5 / ALPHA[layer])
            d = d.reshape(BATCH, 8, 128)
            if down is not None:
                d = d + 0.5 * down
            down = (WEIGHT_VAR / 9.0) * image_blur(d)
        down = down * (2.0 / 3.0)
        for q in range(3):
            x = xa[q, at8, :].reshape(BATCH, 8, 128)
            part = ua[3 + q][at8, :].reshape(BATCH, 8, 128)
            grad[pl.ds(at, BATCH), q * 8 : q * 8 + 8, :] = part + down * x
        return carry

    lax.fori_loop(0, batches, epilogue, 0)


def to_rows(images):
    count = images.shape[0]
    return images.reshape(count, 3, 8, 4, 16, 2).transpose(0, 1, 3, 5, 2, 4).reshape(count, 24, 128)


def from_rows(rows):
    count = rows.shape[0]
    return rows.reshape(count, 3, 4, 2, 8, 16).transpose(0, 1, 4, 2, 5, 3).reshape(count, 3072)


ROWS = 16
COLS = 8
EXTRA = 18
SLOTS = 32 + EXTRA
TABLE = 88
TILES = 6
MESH = pl.DeviceIdType.MESH


def place():
    return lax.axis_index("row"), lax.axis_index("col")


def enter(r, c):
    barrier = pltpu.get_barrier_semaphore()
    me = r * COLS + c
    for i in range(1, ROWS * COLS):
        peer = (me + i) & (ROWS * COLS - 1)
        pl.semaphore_signal(barrier, inc=1, device_id=(peer >> 3, peer & 7), device_id_type=MESH)
    pl.semaphore_wait(barrier, ROWS * COLS - 1)


def ship(go, away, rr, cc, src, dst, send_sem, recv_sem):
    def remote():
        pltpu.make_async_remote_copy(src, dst, send_sem, recv_sem, device_id=(rr, cc), device_id_type=MESH).start()

    def local():
        pltpu.make_async_copy(src, dst, recv_sem).start()

    guarded(go, away, remote)
    if away is not None:
        guarded(go, jnp.logical_not(away), local)


def shipped(go, away, rr, cc, src, dst, send_sem, recv_sem):
    guarded(go, away, lambda: pltpu.make_async_copy(src, src, send_sem).wait())


def guarded(one, two, work):
    conds = [x for x in (one, two) if x is not None]
    if not conds:
        work()
        return
    cond = conds[0] if len(conds) == 1 else jnp.logical_and(*conds)

    @pl.when(cond)
    def _():
        work()


def arrived(dst, recv_sem):
    pltpu.make_async_copy(dst, dst, recv_sem).wait()


def image_routes(r, c):
    e = ((c & 1) << 4) + r
    early = e < 16
    for k in range(4):
        block = 4 * k + (c >> 1)
        for i in range(COLS):
            d = (c + i) & 7
            yield k, block, d, e, (block != r if i == 0 else None)
            rr = (block + 16 - d) & 15
            yield k, rr, d, 32 + e, (rr != r if i == 0 else None)
        rr = (block + 8) & 15
        d = jnp.where(early, e >> 1, 0)
        slot = jnp.where(early, 64 + (e & 1), 50 + e)
        yield k, rr, d, slot, jnp.logical_or(rr != r, d != c)


def slot_count_of(c):
    return jnp.where(c == 0, 32 + EXTRA, 34)


def cot_route(r, c, h, k):
    q = c & 1
    block = 4 * k + (c >> 1)
    dd = block - r
    straight = jnp.logical_or(dd < 8, jnp.logical_and(dd == 8, q == h))
    single = jnp.logical_and(dd >= 0, dd != 8)
    if h == 1:
        single = jnp.logical_and(single, jnp.logical_or(dd != 0, q == 1))
    near = dd < 8
    rr = jnp.where(near, r, block)
    cc = jnp.where(near, dd, 16 - dd) & 7
    slot = jnp.where(near, h * 2 + q, q * 2 + h)
    return dd, single, straight, rr, cc, slot


def tangents(op, r, c, cots, tiles, cot_send, cot_recv, far_send):
    for h in range(2):
        for k in range(4):
            idx = h * 4 + k
            dd, single, straight, rr, cc, slot = cot_route(r, c, h, k)
            src = cots.at[jnp.where(straight, idx, 8 + idx)]
            op(single, dd != c, rr, cc, src, tiles.at[slot], cot_send.at[idx], cot_recv.at[slot])

            @pl.when(dd == 8)
            def _():
                row = jnp.where(straight, r, (r + 8) & 15)
                for i in range(COLS if h == 0 else 1):
                    d = (c + i) & 7 if h == 0 else 0
                    away = jnp.logical_not(straight) if i == 0 else None
                    if h == 1:
                        away = jnp.logical_or(away, c != 0)
                    op(None, away, row, d, src, tiles.at[4 + h], far_send.at[h * 8 + i], cot_recv.at[4 + h])


def partial_routes(r, c):
    for side, block in ((0, r), (1, (r + c) & 15)):
        for half in range(2):
            j = 2 * block + half
            for i in range(ROWS):
                t = (r + i) & 15
                away = (j & 7) != c if i == 0 else None
                yield None, 32 * side + 16 * half + t, t, j & 7, j >> 3, 8 * side + c, away, 32 * side + 16 * half + i
    j = 2 * ((r + 8) & 15)
    for n in range(2):
        t = 2 * c + n
        away = jnp.logical_or(t != r, (j & 7) != c)
        yield None, 64 + n, t, j & 7, j >> 3, 16, away, 64 + n
    j = j + 1
    for i in range(ROWS):
        t = (r + i) & 15
        away = (j & 7) != c if i == 0 else None
        yield c == 0, 66 + t, t, j & 7, j >> 3, 16, away, 66 + i


def tile_route(r, c, slot):
    far = slot >= 4
    bb, qa = slot // 2, slot % 2
    other = (r + 8) & 15 if far else (r + c) & 15
    if far:
        bb = jnp.where(r < 8, qa, 1 - qa)
    ahead = other >= r
    i = jnp.where(ahead, 2 * r + bb, 2 * other + qa)
    j = jnp.where(ahead, 2 * other + qa, 2 * r + bb)
    return i >> 1, j & 7, i & 1, j >> 3


def whole_kernel(mine, cots, image_out, kernel_out, *rest):
    table, tiles, grads, kouts, parts, far = rest[:6]
    img_send, img_recv, cot_send, cot_recv, far_send = rest[6:11]
    part_send, part_recv, tile_send, tile_recv, far_recv = rest[11:16]
    r, c = place()
    enter(r, c)

    def images(op):
        for idx, (k, rr, cc, slot, away) in enumerate(image_routes(r, c)):
            op(None, away, rr, cc, mine.at[k], table.at[slot], img_send.at[idx], img_recv.at[slot])

    images(ship)
    tangents(ship, r, c, cots, tiles, cot_send, cot_recv, far_send)
    for slot in range(66):
        arrived(table.at[slot], img_recv.at[slot])
    for slot in (0, 1, 3, 4):
        arrived(tiles.at[slot], cot_recv.at[slot])

    @pl.when(c != 0)
    def _():
        arrived(tiles.at[2], cot_recv.at[2])
        for slot in range(66, TABLE):
            table[slot] = jnp.zeros((24, 128), jnp.bfloat16)
        tiles[5] = jnp.zeros((16, 128), jnp.bfloat16)

    @pl.when(c == 0)
    def _():
        arrived(tiles.at[5], cot_recv.at[5])
        for slot in range(66, 32 + SLOTS):
            arrived(table.at[slot], img_recv.at[slot])
        for slot in range(32 + SLOTS, TABLE):
            table[slot] = jnp.zeros((24, 128), jnp.bfloat16)
        tiles[2] = jnp.zeros((16, 128), jnp.bfloat16)

    images(shipped)
    tangents(shipped, r, c, cots, tiles, cot_send, cot_recv, far_send)

    compute_kernel(32, plan, table, tiles, kouts, grads, *rest[16:])

    def partials(op):
        for go, slot, rr, cc, k, source, away, sem in partial_routes(r, c):
            op(go, away, rr, cc, grads.at[slot], parts.at[k, source], part_send.at[sem], part_recv.at[k, source])

    def outputs(op):
        for slot in range(TILES):
            rr, cc, h, k = tile_route(r, c, slot)
            go = (None, None, c != 0, None, None, c == 0)[slot]
            if slot == 4:
                dst, sem = far.at[c], far_recv.at[c]
            else:
                dst, sem = kernel_out.at[h * 4 + k], tile_recv.at[h * 4 + k]
            away = jnp.logical_or(rr != r, cc != c)
            op(go, away, rr, cc, kouts.at[slot], dst, tile_send.at[slot], sem)

    partials(ship)
    outputs(ship)

    for h in range(2):
        for k in range(4):
            dd, single, straight, rr, cc, slot = cot_route(r, c, h, k)
            spot = h * 4 + k
            if h == 0:

                @pl.when(dd == 8)
                def _():
                    for d in range(COLS):
                        arrived(far.at[d], far_recv.at[d])
                    total = far[0]
                    for d in range(1, COLS):
                        total = total + far[d]
                    kernel_out[spot] = total

                get = single
            else:
                get = jnp.logical_or(single, dd == 8)

            @pl.when(get)
            def _():
                arrived(kernel_out.at[spot], tile_recv.at[spot])

            unused = dd < 0
            if h == 1:
                unused = jnp.logical_or(unused, jnp.logical_and(dd == 0, (c & 1) == 0))

            @pl.when(unused)
            def _():
                kernel_out[spot] = jnp.zeros((16, 128), jnp.float32)

    for k in range(4):
        for source in range(17):
            arrived(parts.at[k, source], part_recv.at[k, source])
        total = parts[k, 0]
        for source in range(1, 17):
            total = total + parts[k, source]
        image_out[k] = total

    partials(shipped)
    outputs(shipped)


def whole_call(mine, cots):
    whole = pl.BlockSpec(memory_space=pltpu.VMEM)
    dma = pltpu.SemaphoreType.DMA
    vm = lambda *shape: pltpu.VMEM(shape, jnp.float32)
    own, rows = 32, TABLE * 8
    return pl.pallas_call(
        whole_kernel,
        out_shape=(
            jax.ShapeDtypeStruct((4, 24, 128), jnp.float32),
            jax.ShapeDtypeStruct((8, 16, 128), jnp.float32),
        ),
        in_specs=[whole, whole],
        out_specs=(whole, whole),
        scratch_shapes=[
            pltpu.VMEM((TABLE, 24, 128), jnp.bfloat16),
            pltpu.VMEM((TILES, 16, 128), jnp.bfloat16),
            vm(TABLE, 24, 128),
            vm(TILES, 16, 128),
            vm(4, 17, 24, 128),
            vm(8, 16, 128),
        ]
        + [dma((68,)), dma((32 + SLOTS,)), dma((8,)), dma((TILES,)), dma((16,))]
        + [dma((32 + SLOTS,)), dma((4, 17)), dma((TILES,)), dma((8,)), dma((8,))]
        + [vm(3, rows, 128)] * 3
        + [vm(3, 8, own, 128)] * 3
        + [vm(8, own, 128)] * 6
        + [vm(rows, 128)] * 6
        + ([vm(8, 16, 128)] * 5 + [vm(64, 128)] * 6) * 2,
        compiler_params=pltpu.CompilerParams(
            collective_id=0, has_side_effects=True, vmem_limit_bytes=56 * 1024 * 1024
        ),
    )(mine, cots)


def plan():
    r, c = place()

    def unit_of(u):
        first = c == 0
        n = u - jnp.where(first, 48, 64)
        main = n < 0
        e = jnp.where(n < 2, 2 * c + n, 14 + n)
        half = jnp.where(r < 8, e // 16, 1 - e // 16)
        short = jnp.logical_and(first, u < 16)
        v = jnp.where(first, u + 16, u)
        slot = jnp.where(main, jnp.where(short, u, v // 2), 32 + n)
        bb = jnp.where(main, jnp.where(short, 0, v % 2), half)
        tile = jnp.where(main, bb * 2 + slot // 16, 4 + e // 16)
        return slot, bb, tile, jnp.where(main, slot, e) % 16

    return 66, slot_count_of(c), unit_of


def body(images, cotangent):
    r, c = place()
    mine = to_rows(images.reshape(4, 3072))
    cot = cotangent.reshape(2, 16, 4, 16).transpose(0, 2, 1, 3).reshape(8, 16, 16)
    cots = jnp.concatenate([cot, cot.swapaxes(1, 2)])
    cots = jnp.pad(cots, ((0, 0), (0, 0), (0, 112)))
    image_out, kernel_out = whole_call(mine, cots)
    out = kernel_out[:, :, :16].reshape(2, 4, 16, 16)
    half = jnp.arange(2)[:, None, None, None]
    k = jnp.arange(4)[None, :, None, None]
    dd = 4 * k + c // 2 - r
    straight = jnp.logical_or(dd < 8, jnp.logical_and(dd == 8, half == c % 2))
    out = jnp.where(straight, out, out.swapaxes(2, 3))
    kernel = out.transpose(0, 2, 1, 3).reshape(2, 16, 4, 1, 16)
    return kernel, from_rows(image_out).reshape(4, 1, 1, 3072)


def solution(mesh):
    return jax.shard_map(
        body,
        mesh=mesh,
        in_specs=(P(None, "col", "row", None), P("row", None, None, "col", None)),
        out_specs=(P("row", None, None, "col", None), P(None, "col", "row", None)),
        check_vma=False,
    )
```

```python
import math

import jax
import jax.numpy as jnp
from jax import lax
from jax.experimental import pallas as pl
from jax.experimental.pallas import tpu as pltpu
from jax.sharding import PartitionSpec as P

WEIGHT_VAR = 2.0
BIAS_VAR = 0.1
LAYERS = 3
ALPHA = [WEIGHT_VAR / 27.0]
for _ in range(LAYERS - 1):
    ALPHA.append(ALPHA[-1] * WEIGHT_VAR / 9.0)
BIAS = [BIAS_VAR / a for a in ALPHA]
ASIN = [
    a / (2.0 * math.pi)
    for a in (
        -0.10520251251688581,
        1.0690300997862225,
        0.9916991797412131,
        -0.4865441702586394,
        0.1018140487237715,
    )
]
TINY = 1e-30
BATCH = 8
HALVES = 2


def lane_masks(shape):
    lane = lax.broadcasted_iota(jnp.int32, shape, len(shape) - 1)
    f = jnp.float32
    return (
        (lane % 16 != 0).astype(f),
        (lane % 16 != 15).astype(f),
        (lane >= 16).astype(f),
        (lane < 112).astype(f),
    )


def compute_kernel(n_own, plan, landed, finished, img, cot, kout, grad, xa, ra, ta, xb, rb, tb, *rest):
    ub, ua, save = rest[:6], rest[6:12], (rest[12:23], rest[23:34])
    f32 = jnp.float32
    unit_count, slot_count, unit_of = plan()
    left, right, upper, lower = lane_masks((16, 128))

    row3 = lax.broadcasted_iota(jnp.int32, (BATCH, 8, 128), 1)
    masks3 = lane_masks((BATCH, 8, 128))

    def image_blur(v):
        even = row3 % 2 == 0
        mate = jnp.where(even, pltpu.roll(v, 7, 1), pltpu.roll(v, 1, 1))
        side = jnp.where(even, masks3[0] * pltpu.roll(mate, 1, 2), masks3[1] * pltpu.roll(mate, 127, 2))
        h = v + mate + side
        above = pltpu.roll(h, 2, 1)
        below = pltpu.roll(h, 6, 1)
        above = jnp.where(row3 < 2, masks3[2] * pltpu.roll(above, 16, 2), above)
        below = jnp.where(row3 >= 6, masks3[3] * pltpu.roll(below, 112, 2), below)
        return h + above + below

    def prologue(step, carry):
        at = pl.multiple_of(step * BATCH, BATCH)
        at8 = pl.ds(pl.multiple_of(step * BATCH * 8, BATCH * 8), BATCH * 8)
        val = img[pl.ds(at, BATCH)].astype(f32)
        var = jnp.zeros((BATCH, 8, 128), f32)
        for ch in range(3):
            x = val[:, ch * 8 : ch * 8 + 8, :]
            xa[ch, at8, :] = x.reshape(BATCH * 8, 128)
            var = var + x * x
        var = var * (1.0 / 3.0)
        for layer in range(LAYERS):
            area = (WEIGHT_VAR / 9.0) * image_blur(var) + BIAS_VAR
            inv = lax.rsqrt(area)
            ra[layer, at8, :] = (inv * math.sqrt(ALPHA[layer])).reshape(BATCH * 8, 128)
            ta[layer, at8, :] = (
                area * inv * (1.0 / math.sqrt(2.0 * math.pi * ALPHA[layer]))
            ).reshape(BATCH * 8, 128)
            var = 0.5 * area
        for k in range(6):
            ua[k][at8, :] = jnp.zeros((BATCH * 8, 128), f32)
        return carry

    more = slot_count > 34

    def fetched(step, carry):
        landed(step)
        return prologue(step, carry)

    lax.fori_loop(0, 9, fetched, 0)

    @pl.when(more)
    def _():
        lax.fori_loop(9, TABLE // BATCH, fetched, 0)


    for group in range(n_own // 8):
        for s in range(8):
            rows = pl.ds(group * 64 + s, 8, stride=8)
            part = slice(group * 8, group * 8 + 8)
            for q in range(3):
                xb[q, s, part, :] = xa[q, rows, :]
                rb[q, s, part, :] = ra[q, rows, :]
                tb[q, s, part, :] = ta[q, rows, :]
    for k in range(6):
        ub[k][...] = jnp.zeros_like(ub[k])
    kout[...] = jnp.zeros_like(kout)

    def across(v):
        out = [None] * 8
        for p in range(0, 8, 2):
            mid = v[p] + v[p + 1]
            out[p] = mid + left * pltpu.roll(v[p + 1], 1, 1)
            out[p + 1] = mid + right * pltpu.roll(v[p], 127, 1)
        return out

    def vertical(h, bias):
        w = [None] * 8
        for sx in range(2):
            top = upper * pltpu.roll(h[6 + sx], 16, 1)
            bottom = lower * pltpu.roll(h[sx], 112, 1)
            one = h[sx] + h[2 + sx]
            two = h[4 + sx] + h[6 + sx]
            if bias is not None:
                one = one + bias
                two = two + bias
            w[sx] = one + top
            w[2 + sx] = one + h[4 + sx]
            w[4 + sx] = h[2 + sx] + two
            w[6 + sx] = two + bottom
        return w

    lane16 = lax.broadcasted_iota(jnp.int32, (16, 128), 1)
    ORDER = (0, 7, 1, 6, 2, 5, 3, 4)

    def ready(u):
        slot, bb, tile, lane = unit_of(u)
        base = pl.multiple_of((n_own + slot) * 8, 8)
        own = pl.ds(pl.multiple_of(bb * 16, 16), 16)
        return base, own, tile, lane

    def arow(ref, q, base, s):
        return ref[q, pl.ds(base + s, 1), :]

    def fold(uacc, k, base):
        total = uacc[k][pl.ds(0, 8, stride=8), :]
        for b in range(1, 8):
            total = total + uacc[k][pl.ds(b, 8, stride=8), :]
        ua[k][pl.ds(base, 8), :] += total

    def tally(uacc, k, s, own, e_own, e_slot):
        ub[k][s, own, :] += e_own
        uacc[k][s * 8 : s * 8 + 8, :] = e_slot[:8] + e_slot[8:]

    def forward(u, saved):
        sg1, sz1, sg2, sz2, sh, *uacc = saved
        base, own, tile, lane = ready(u)
        h = [None] * 8
        for s in ORDER:
            x = xb[0, s, own, :] * arow(xa, 0, base, s)
            x = x + xb[1, s, own, :] * arow(xa, 1, base, s)
            x = x + xb[2, s, own, :] * arow(xa, 2, base, s)
            h[s] = x
        h = across(h)
        weight = jnp.where(lane16 == lane, cot[tile].astype(f32), 0.0)
        weight = jnp.sum(weight, axis=1, keepdims=True) * (WEIGHT_VAR * ALPHA[2] / 1024.0)
        weight = jnp.broadcast_to(weight, (16, 128))
        total = None
        for layer in range(LAYERS):
            w = vertical(h, BIAS[layer])
            h = [None] * 8
            for s in ORDER:
                c = (w[s] * rb[layer, s, own, :]) * arow(ra, layer, base, s)
                y = jnp.maximum(1.0 - c * c, TINY)
                sine = y * lax.rsqrt(y)
                v = lax.rsqrt(1.0 + sine)
                poly = ASIN[4] * v + ASIN[3]
                for k in range(2, -1, -1):
                    poly = poly * v + ASIN[k]
                g = c * poly + 0.25
                z = (sine * tb[layer, s, own, :]) * arow(ta, layer, base, s)
                f = w[s] * g + z
                if layer < LAYERS - 1:
                    (sg1, sg2)[layer][s] = g
                    (sz1, sz2)[layer][s] = z
                    h[s] = f
                else:
                    total = f if total is None else total + f
                    e = weight * z
                    tally(uacc, layer, s, own, e, e)
                    h[s] = weight * g
            h = across(h)
        for s in range(8):
            sh[s] = h[s]
        fold(uacc, LAYERS - 1, base)
        value = jnp.sum(total, axis=1, keepdims=True) * (WEIGHT_VAR * ALPHA[2] / 1024.0) + BIAS_VAR
        kout[tile] = jnp.where(lane16 == lane, value, kout[tile])

    def backward(u, saved):
        sg1, sz1, sg2, sz2, sh, *uacc = saved
        base, own, tile, lane = ready(u)
        h = [sh[s] for s in range(8)]
        for layer in range(LAYERS - 2, -1, -1):
            w = vertical(h, None)
            h = [None] * 8
            for s in ORDER:
                e = w[s] * (sz1, sz2)[layer][s]
                tally(uacc, layer, s, own, e, e)
                h[s] = w[s] * (sg1, sg2)[layer][s]
            h = across(h)
            fold(uacc, layer, base)
        w = vertical(h, None)
        for s in range(8):
            for q in range(3):
                tally(uacc, 3 + q, s, own, w[s] * arow(xa, q, base, s), w[s] * xb[q, s, own, :])
        for q in range(3):
            fold(uacc, 3 + q, base)

    forward(jnp.int32(0), save[0])
    forward(jnp.int32(1), save[1])

    def pair(i, carry):
        backward(2 * i, save[0])
        forward(2 * i + 2, save[0])
        backward(2 * i + 1, save[1])
        forward(2 * i + 3, save[1])
        return carry

    def epilogue(step, carry):
        at = pl.multiple_of(step * BATCH, BATCH)
        at8 = pl.ds(pl.multiple_of(step * BATCH * 8, BATCH * 8), BATCH * 8)
        down = None
        for layer in range(LAYERS - 1, -1, -1):
            r = ra[layer, at8, :]
            d = ua[layer][at8, :] * (r * r) * (0.5 / ALPHA[layer])
            d = d.reshape(BATCH, 8, 128)
            if down is not None:
                d = d + 0.5 * down
            down = (WEIGHT_VAR / 9.0) * image_blur(d)
        down = down * (2.0 / 3.0)
        for q in range(3):
            x = xa[q, at8, :].reshape(BATCH, 8, 128)
            part = ua[3 + q][at8, :].reshape(BATCH, 8, 128)
            grad[pl.ds(at, BATCH), q * 8 : q * 8 + 8, :] = part + down * x
        return carry

    def segment(n, carry):
        lax.fori_loop(8 * n, 8 * n + 8, pair, 0)
        epilogue(4 + n, 0)
        finished(4 + n)
        return carry

    lax.fori_loop(0, 4, segment, 0)
    backward(jnp.int32(unit_count - 2), save[0])
    backward(jnp.int32(unit_count - 1), save[1])

    for group in range(n_own // 8):
        for s in range(8):
            rows = pl.ds(group * 64 + s, 8, stride=8)
            for k in range(6):
                ua[k][rows, :] = ub[k][s, group * 8 : group * 8 + 8, :]

    def last(step, carry):
        epilogue(step, 0)
        finished(step)
        return carry

    lax.fori_loop(0, 4, last, 0)
    last(8, 0)

    @pl.when(more)
    def _():
        lax.fori_loop(9, TABLE // BATCH, last, 0)


def to_rows(images):
    count = images.shape[0]
    return images.reshape(count, 3, 8, 4, 16, 2).transpose(0, 1, 3, 5, 2, 4).reshape(count, 24, 128)


def from_rows(rows):
    count = rows.shape[0]
    return rows.reshape(count, 3, 4, 2, 8, 16).transpose(0, 1, 4, 2, 5, 3).reshape(count, 3072)


ROWS = 16
COLS = 8
EXTRA = 18
SLOTS = 32 + EXTRA
TABLE = 88
TILES = 6
MESH = pl.DeviceIdType.MESH


def place():
    return lax.axis_index("row"), lax.axis_index("col")


def greet(r, c):
    barrier = pltpu.get_barrier_semaphore()
    x, y, z = (r >> 1) & 3, c >> 1, ((c & 1) << 1) + (r >> 3)
    xs = [((x + d) & 3) << 1 for d in range(4)]
    ys = [((y + d) & 3) << 1 for d in range(4)]
    zs = [((z + d) & 3) for d in range(4)]
    cores = [r & 1, 1 - (r & 1)]
    far = lambda o: sum(min(d, 4 - d) for d in o[:3]) + 0.1 * o[3]
    steps = [(i, j, k, l) for i in range(4) for j in range(4) for k in range(4) for l in range(2)]
    for i, j, k, l in sorted(steps, key=far, reverse=True)[:-1]:
        rr = ((zs[k] & 1) << 3) + xs[i] + cores[l]
        pl.semaphore_signal(barrier, inc=1, device_id=(rr, ys[j] + (zs[k] >> 1)), device_id_type=MESH)


def enter():
    pl.semaphore_wait(pltpu.get_barrier_semaphore(), ROWS * COLS - 1)


def ship(go, away, rr, cc, src, dst, send_sem, recv_sem):
    def remote():
        pltpu.make_async_remote_copy(src, dst, send_sem, recv_sem, device_id=(rr, cc), device_id_type=MESH).start()

    def local():
        pltpu.make_async_copy(src, dst, recv_sem).start()

    guarded(go, away, remote)
    if away is not None:
        guarded(go, jnp.logical_not(away), local)


def shipped(go, away, rr, cc, src, dst, send_sem, recv_sem):
    guarded(go, away, lambda: pltpu.make_async_copy(src, src, send_sem).wait())


def guarded(one, two, work):
    conds = [x for x in (one, two) if x is not None]
    if not conds:
        work()
        return
    cond = conds[0] if len(conds) == 1 else jnp.logical_and(*conds)

    @pl.when(cond)
    def _():
        work()


def arrived(dst, recv_sem):
    pltpu.make_async_copy(dst, dst, recv_sem).wait()


def image_routes(r, c):
    e = ((c & 1) << 4) + r
    early = e < 16
    for k in range(4):
        block = 4 * k + (c >> 1)
        for i in range(COLS):
            d = (c + i) & 7
            yield k, block, d, e, (block != r if i == 0 else None)
            rr = (block + 16 - d) & 15
            yield k, rr, d, 32 + e, (rr != r if i == 0 else None)
        rr = (block + 8) & 15
        d = jnp.where(early, e >> 1, 0)
        slot = jnp.where(early, 64 + (e & 1), 50 + e)
        yield k, rr, d, slot, jnp.logical_or(rr != r, d != c)


def slot_count_of(c):
    return jnp.where(c == 0, 32 + EXTRA, 34)


def cot_route(r, c, h, k):
    q = c & 1
    block = 4 * k + (c >> 1)
    dd = block - r
    straight = jnp.logical_or(dd < 8, jnp.logical_and(dd == 8, q == h))
    single = jnp.logical_and(dd >= 0, dd != 8)
    if h == 1:
        single = jnp.logical_and(single, jnp.logical_or(dd != 0, q == 1))
    near = dd < 8
    rr = jnp.where(near, r, block)
    cc = jnp.where(near, dd, 16 - dd) & 7
    slot = jnp.where(near, h * 2 + q, q * 2 + h)
    return dd, single, straight, rr, cc, slot


def tangents(op, r, c, cots, tiles, cot_send, cot_recv, far_send):
    for h in range(2):
        for k in range(4):
            idx = h * 4 + k
            dd, single, straight, rr, cc, slot = cot_route(r, c, h, k)
            src = cots.at[jnp.where(straight, idx, 8 + idx)]
            op(single, dd != c, rr, cc, src, tiles.at[slot], cot_send.at[idx], cot_recv.at[slot])

            @pl.when(dd == 8)
            def _():
                row = jnp.where(straight, r, (r + 8) & 15)
                for i in range(COLS if h == 0 else 1):
                    d = (c + i) & 7 if h == 0 else 0
                    away = jnp.logical_not(straight) if i == 0 else None
                    if h == 1:
                        away = jnp.logical_or(away, c != 0)
                    op(None, away, row, d, src, tiles.at[4 + h], far_send.at[h * 8 + i], cot_recv.at[4 + h])


def partial_route(r, c, batch, n):
    slot = batch * BATCH + n
    main = batch < 8
    own = batch < 4
    x = slot - 64
    e = jnp.where(main, slot & 31, jnp.where(x < 2, 2 * c + x, 14 + x))
    block = jnp.where(own, r, jnp.where(main, r + c, r + 8) & 15)
    j = 2 * block + (e >> 4)
    source = jnp.where(own, c, jnp.where(main, 8 + c, 16))
    return slot, e & 15, j & 7, j >> 3, source


def tile_route(r, c, slot):
    far = slot >= 4
    bb, qa = slot // 2, slot % 2
    other = (r + 8) & 15 if far else (r + c) & 15
    if far:
        bb = jnp.where(r < 8, qa, 1 - qa)
    ahead = other >= r
    i = jnp.where(ahead, 2 * r + bb, 2 * other + qa)
    j = jnp.where(ahead, 2 * other + qa, 2 * r + bb)
    return i >> 1, j & 7, i & 1, j >> 3


def whole_kernel(mine, cots, image_out, kernel_out, *rest):
    table, tiles, grads, kouts, parts, far = rest[:6]
    img_send, img_recv, cot_send, cot_recv, far_send = rest[6:11]
    part_send, part_recv, tile_send, tile_recv, far_recv = rest[11:16]
    r, c = place()
    greet(r, c)
    enter()

    def images(op):
        for idx, (k, rr, cc, slot, away) in enumerate(image_routes(r, c)):
            op(None, away, rr, cc, mine.at[k], table.at[slot], img_send.at[idx], img_recv.at[slot])

    images(ship)
    tangents(ship, r, c, cots, tiles, cot_send, cot_recv, far_send)
    for slot in (0, 1, 3, 4):
        arrived(tiles.at[slot], cot_recv.at[slot])

    @pl.when(c != 0)
    def _():
        arrived(tiles.at[2], cot_recv.at[2])
        tiles[5] = jnp.zeros((16, 128), jnp.bfloat16)
        for slot in range(66, 72):
            table[slot] = jnp.zeros((24, 128), jnp.bfloat16)

    @pl.when(c == 0)
    def _():
        arrived(tiles.at[5], cot_recv.at[5])
        tiles[2] = jnp.zeros((16, 128), jnp.bfloat16)
        for slot in range(32 + SLOTS, TABLE):
            table[slot] = jnp.zeros((24, 128), jnp.bfloat16)

    def used(batch, n):
        slot = batch * BATCH + n
        return jnp.logical_or(slot < 66, jnp.logical_and(c == 0, slot < 32 + SLOTS))

    def landed(batch):
        for n in range(BATCH):
            slot = batch * BATCH + n
            guarded(used(batch, n), None, lambda: arrived(table.at[slot], img_recv.at[slot]))

    def partials(op, batch):
        for n in range(BATCH):
            slot, rr, cc, k, source = partial_route(r, c, batch, n)
            away = jnp.logical_or(rr != r, cc != c)
            op(used(batch, n), away, rr, cc, grads.at[slot], parts.at[k, source], part_send.at[slot], part_recv.at[k, source])

    compute_kernel(
        32, plan, landed, lambda batch: partials(ship, batch), table, tiles, kouts, grads, *rest[16:]
    )

    def outputs(op):
        for slot in range(TILES):
            rr, cc, h, k = tile_route(r, c, slot)
            go = (None, None, c != 0, None, None, c == 0)[slot]
            if slot == 4:
                dst, sem = far.at[c], far_recv.at[c]
            else:
                dst, sem = kernel_out.at[h * 4 + k], tile_recv.at[h * 4 + k]
            away = jnp.logical_or(rr != r, cc != c)
            op(go, away, rr, cc, kouts.at[slot], dst, tile_send.at[slot], sem)

    outputs(ship)

    for h in range(2):
        for k in range(4):
            dd, single, straight, rr, cc, slot = cot_route(r, c, h, k)
            spot = h * 4 + k
            if h == 0:

                @pl.when(dd == 8)
                def _():
                    for d in range(COLS):
                        arrived(far.at[d], far_recv.at[d])
                    total = far[0]
                    for d in range(1, COLS):
                        total = total + far[d]
                    kernel_out[spot] = total

                get = single
            else:
                get = jnp.logical_or(single, dd == 8)

            @pl.when(get)
            def _():
                arrived(kernel_out.at[spot], tile_recv.at[spot])

            unused = dd < 0
            if h == 1:
                unused = jnp.logical_or(unused, jnp.logical_and(dd == 0, (c & 1) == 0))

            @pl.when(unused)
            def _():
                kernel_out[spot] = jnp.zeros((16, 128), jnp.float32)

    for k in range(4):
        for source in range(17):
            arrived(parts.at[k, source], part_recv.at[k, source])
        total = parts[k, 0]
        for source in range(1, 17):
            total = total + parts[k, source]
        image_out[k] = total

    images(shipped)
    tangents(shipped, r, c, cots, tiles, cot_send, cot_recv, far_send)
    outputs(shipped)

    def settle(batch, carry):
        partials(shipped, batch)
        return carry

    lax.fori_loop(0, TABLE // BATCH, settle, 0)


def whole_call(mine, cots):
    whole = pl.BlockSpec(memory_space=pltpu.VMEM)
    dma = pltpu.SemaphoreType.DMA
    vm = lambda *shape: pltpu.VMEM(shape, jnp.float32)
    own, rows = 32, TABLE * 8
    return pl.pallas_call(
        whole_kernel,
        out_shape=(
            jax.ShapeDtypeStruct((4, 24, 128), jnp.float32),
            jax.ShapeDtypeStruct((8, 16, 128), jnp.float32),
        ),
        in_specs=[whole, whole],
        out_specs=(whole, whole),
        scratch_shapes=[
            pltpu.VMEM((TABLE, 24, 128), jnp.bfloat16),
            pltpu.VMEM((TILES, 16, 128), jnp.bfloat16),
            vm(TABLE, 24, 128),
            vm(TILES, 16, 128),
            vm(4, 17, 24, 128),
            vm(8, 16, 128),
        ]
        + [dma((68,)), dma((32 + SLOTS,)), dma((8,)), dma((TILES,)), dma((16,))]
        + [dma((32 + SLOTS,)), dma((4, 17)), dma((TILES,)), dma((8,)), dma((8,))]
        + [vm(3, rows, 128)] * 3
        + [vm(3, 8, own, 128)] * 3
        + [vm(8, own, 128)] * 6
        + [vm(rows, 128)] * 6
        + ([vm(8, 16, 128)] * 5 + [vm(64, 128)] * 6) * 2,
        compiler_params=pltpu.CompilerParams(
            collective_id=0, has_side_effects=True, vmem_limit_bytes=56 * 1024 * 1024
        ),
    )(mine, cots)


def plan():
    r, c = place()

    def unit_of(u):
        first = c == 0
        n = u - jnp.where(first, 48, 64)
        main = n < 0
        e = jnp.where(n < 2, 2 * c + n, 14 + n)
        half = jnp.where(r < 8, e // 16, 1 - e // 16)
        short = jnp.logical_and(first, u < 16)
        v = jnp.where(first, u + 16, u)
        slot = jnp.where(main, jnp.where(short, u, v // 2), 32 + n)
        bb = jnp.where(main, jnp.where(short, 0, v % 2), half)
        tile = jnp.where(main, bb * 2 + slot // 16, 4 + e // 16)
        return slot, bb, tile, jnp.where(main, slot, e) % 16

    return 66, slot_count_of(c), unit_of


def body(images, cotangent):
    r, c = place()
    mine = to_rows(images.reshape(4, 3072))
    cot = cotangent.reshape(2, 16, 4, 16).transpose(0, 2, 1, 3).reshape(8, 16, 16)
    cots = jnp.concatenate([cot, cot.swapaxes(1, 2)])
    cots = jnp.pad(cots, ((0, 0), (0, 0), (0, 112)))
    image_out, kernel_out = whole_call(mine, cots)
    out = kernel_out[:, :, :16].reshape(2, 4, 16, 16)
    half = jnp.arange(2)[:, None, None, None]
    k = jnp.arange(4)[None, :, None, None]
    dd = 4 * k + c // 2 - r
    straight = jnp.logical_or(dd < 8, jnp.logical_and(dd == 8, half == c % 2))
    out = jnp.where(straight, out, out.swapaxes(2, 3))
    kernel = out.transpose(0, 2, 1, 3).reshape(2, 16, 4, 1, 16)
    return kernel, from_rows(image_out).reshape(4, 1, 1, 3072)


def solution(mesh):
    return jax.shard_map(
        body,
        mesh=mesh,
        in_specs=(P(None, "col", "row", None), P("row", None, None, "col", None)),
        out_specs=(P("row", None, None, "col", None), P(None, "col", "row", None)),
        check_vma=False,
    )
```

```python
import math

import jax
import jax.numpy as jnp
from jax import lax
from jax.experimental import pallas as pl
from jax.experimental.pallas import tpu as pltpu
from jax.sharding import PartitionSpec as P

WEIGHT_VAR = 2.0
BIAS_VAR = 0.1
LAYERS = 3
ALPHA = [WEIGHT_VAR / 27.0]
for _ in range(LAYERS - 1):
    ALPHA.append(ALPHA[-1] * WEIGHT_VAR / 9.0)
BIAS = [BIAS_VAR / a for a in ALPHA]
ASIN = [
    a / (2.0 * math.pi)
    for a in (
        -0.10520251251688581,
        1.0690300997862225,
        0.9916991797412131,
        -0.4865441702586394,
        0.1018140487237715,
    )
]
TINY = 1e-30
BATCH = 8
HALVES = 2


def lane_masks(shape):
    lane = lax.broadcasted_iota(jnp.int32, shape, len(shape) - 1)
    f = jnp.float32
    return (
        (lane % 16 != 0).astype(f),
        (lane % 16 != 15).astype(f),
        (lane >= 16).astype(f),
        (lane < 112).astype(f),
    )


def compute_kernel(n_own, plan, landed, finished, img, cot, kout, grad, xa, ra, ta, xb, rb, tb, *rest):
    ub, ua, save = rest[:6], rest[6:12], (rest[12:23], rest[23:34])
    f32 = jnp.float32
    unit_count, slot_count, unit_of, turned = plan()
    left, right, upper, lower = lane_masks((16, 128))

    row3 = lax.broadcasted_iota(jnp.int32, (BATCH, 8, 128), 1)
    masks3 = lane_masks((BATCH, 8, 128))

    def image_blur(v):
        even = row3 % 2 == 0
        mate = jnp.where(even, pltpu.roll(v, 7, 1), pltpu.roll(v, 1, 1))
        side = jnp.where(even, masks3[0] * pltpu.roll(mate, 1, 2), masks3[1] * pltpu.roll(mate, 127, 2))
        h = v + mate + side
        above = pltpu.roll(h, 2, 1)
        below = pltpu.roll(h, 6, 1)
        above = jnp.where(row3 < 2, masks3[2] * pltpu.roll(above, 16, 2), above)
        below = jnp.where(row3 >= 6, masks3[3] * pltpu.roll(below, 112, 2), below)
        return h + above + below

    def prologue(step, carry):
        at = pl.multiple_of(step * BATCH, BATCH)
        at8 = pl.ds(pl.multiple_of(step * BATCH * 8, BATCH * 8), BATCH * 8)
        val = img[pl.ds(at, BATCH)].astype(f32)
        var = jnp.zeros((BATCH, 8, 128), f32)
        for ch in range(3):
            x = val[:, ch * 8 : ch * 8 + 8, :]
            xa[ch, at8, :] = x.reshape(BATCH * 8, 128)
            var = var + x * x
        var = var * (1.0 / 3.0)
        for layer in range(LAYERS):
            area = (WEIGHT_VAR / 9.0) * image_blur(var) + BIAS_VAR
            inv = lax.rsqrt(area)
            ra[layer, at8, :] = (inv * math.sqrt(ALPHA[layer])).reshape(BATCH * 8, 128)
            ta[layer, at8, :] = (
                area * inv * (1.0 / math.sqrt(2.0 * math.pi * ALPHA[layer]))
            ).reshape(BATCH * 8, 128)
            var = 0.5 * area
        for k in range(6):
            ua[k][at8, :] = jnp.zeros((BATCH * 8, 128), f32)
        return carry

    more = slot_count > 34

    def fetched(step, carry):
        landed(step)
        return prologue(step, carry)

    lax.fori_loop(0, 9, fetched, 0)

    @pl.when(more)
    def _():
        lax.fori_loop(9, TABLE // BATCH, fetched, 0)


    for group in range(n_own // 8):
        for s in range(8):
            rows = pl.ds(group * 64 + s, 8, stride=8)
            part = slice(group * 8, group * 8 + 8)
            for q in range(3):
                xb[q, s, part, :] = xa[q, rows, :]
                rb[q, s, part, :] = ra[q, rows, :]
                tb[q, s, part, :] = ta[q, rows, :]
    for k in range(6):
        ub[k][...] = jnp.zeros_like(ub[k])
    kout[...] = jnp.zeros_like(kout)

    def across(v):
        out = [None] * 8
        for p in range(0, 8, 2):
            mid = v[p] + v[p + 1]
            out[p] = mid + left * pltpu.roll(v[p + 1], 1, 1)
            out[p + 1] = mid + right * pltpu.roll(v[p], 127, 1)
        return out

    def vertical(h, bias):
        w = [None] * 8
        for sx in range(2):
            top = upper * pltpu.roll(h[6 + sx], 16, 1)
            bottom = lower * pltpu.roll(h[sx], 112, 1)
            one = h[sx] + h[2 + sx]
            two = h[4 + sx] + h[6 + sx]
            if bias is not None:
                one = one + bias
                two = two + bias
            w[sx] = one + top
            w[2 + sx] = one + h[4 + sx]
            w[4 + sx] = h[2 + sx] + two
            w[6 + sx] = two + bottom
        return w

    lane16 = lax.broadcasted_iota(jnp.int32, (16, 128), 1)
    row16 = lax.broadcasted_iota(jnp.int32, (16, 128), 0)
    ORDER = (0, 7, 1, 6, 2, 5, 3, 4)

    def ready(u):
        slot, bb, tile, lane = unit_of(u)
        base = pl.multiple_of((n_own + slot) * 8, 8)
        own = pl.ds(pl.multiple_of(bb * 16, 16), 16)
        return base, own, tile, lane

    def arow(ref, q, base, s):
        return ref[q, pl.ds(base + s, 1), :]

    def fold(uacc, k, base):
        total = uacc[k][pl.ds(0, 8, stride=8), :]
        for b in range(1, 8):
            total = total + uacc[k][pl.ds(b, 8, stride=8), :]
        ua[k][pl.ds(base, 8), :] += total

    def tally(uacc, k, s, own, e_own, e_slot):
        ub[k][s, own, :] += e_own
        uacc[k][s * 8 : s * 8 + 8, :] = e_slot[:8] + e_slot[8:]

    def forward(u, saved):
        sg1, sz1, sg2, sz2, sh, *uacc = saved
        base, own, tile, lane = ready(u)
        h = [None] * 8
        for s in ORDER:
            x = xb[0, s, own, :] * arow(xa, 0, base, s)
            x = x + xb[1, s, own, :] * arow(xa, 1, base, s)
            x = x + xb[2, s, own, :] * arow(xa, 2, base, s)
            h[s] = x
        h = across(h)
        spin = turned(u)
        row = cot[pl.ds(tile * 16 + lane, 1), :]
        source = jnp.where(spin, jnp.broadcast_to(row, (16, 128)), cot[pl.ds(pl.multiple_of(tile * 16, 16), 16), :])
        weight = jnp.where(lane16 == jnp.where(spin, row16, lane), source, 0.0)
        weight = jnp.sum(weight, axis=1, keepdims=True) * (WEIGHT_VAR * ALPHA[2] / 1024.0)
        weight = jnp.broadcast_to(weight, (16, 128))
        total = None
        for layer in range(LAYERS):
            w = vertical(h, BIAS[layer])
            h = [None] * 8
            for s in ORDER:
                c = (w[s] * rb[layer, s, own, :]) * arow(ra, layer, base, s)
                y = jnp.maximum(1.0 - c * c, TINY)
                sine = y * lax.rsqrt(y)
                v = lax.rsqrt(1.0 + sine)
                poly = ASIN[4] * v + ASIN[3]
                for k in range(2, -1, -1):
                    poly = poly * v + ASIN[k]
                g = c * poly + 0.25
                z = (sine * tb[layer, s, own, :]) * arow(ta, layer, base, s)
                f = w[s] * g + z
                if layer < LAYERS - 1:
                    (sg1, sg2)[layer][s] = g
                    (sz1, sz2)[layer][s] = z
                    h[s] = f
                else:
                    total = f if total is None else total + f
                    e = weight * z
                    tally(uacc, layer, s, own, e, e)
                    h[s] = weight * g
            h = across(h)
        for s in range(8):
            sh[s] = h[s]
        fold(uacc, LAYERS - 1, base)
        value = jnp.sum(total, axis=1, keepdims=True) * (WEIGHT_VAR * ALPHA[2] / 1024.0) + BIAS_VAR
        value = jnp.broadcast_to(value, (16, 128))
        flat = jnp.sum(jnp.where(lane16 == row16, value, 0.0), axis=0, keepdims=True)
        value = jnp.where(spin, jnp.broadcast_to(flat, (16, 128)), value)
        kout[tile] = jnp.where(jnp.where(spin, row16, lane16) == lane, value, kout[tile])

    def backward(u, saved):
        sg1, sz1, sg2, sz2, sh, *uacc = saved
        base, own, tile, lane = ready(u)
        h = [sh[s] for s in range(8)]
        for layer in range(LAYERS - 2, -1, -1):
            w = vertical(h, None)
            h = [None] * 8
            for s in ORDER:
                e = w[s] * (sz1, sz2)[layer][s]
                tally(uacc, layer, s, own, e, e)
                h[s] = w[s] * (sg1, sg2)[layer][s]
            h = across(h)
            fold(uacc, layer, base)
        w = vertical(h, None)
        for s in range(8):
            for q in range(3):
                tally(uacc, 3 + q, s, own, w[s] * arow(xa, q, base, s), w[s] * xb[q, s, own, :])
        for q in range(3):
            fold(uacc, 3 + q, base)

    forward(jnp.int32(0), save[0])
    forward(jnp.int32(1), save[1])

    def pair(i, carry):
        backward(2 * i, save[0])
        forward(2 * i + 2, save[0])
        backward(2 * i + 1, save[1])
        forward(2 * i + 3, save[1])
        return carry

    def epilogue(step, carry):
        at = pl.multiple_of(step * BATCH, BATCH)
        at8 = pl.ds(pl.multiple_of(step * BATCH * 8, BATCH * 8), BATCH * 8)
        down = None
        for layer in range(LAYERS - 1, -1, -1):
            r = ra[layer, at8, :]
            d = ua[layer][at8, :] * (r * r) * (0.5 / ALPHA[layer])
            d = d.reshape(BATCH, 8, 128)
            if down is not None:
                d = d + 0.5 * down
            down = (WEIGHT_VAR / 9.0) * image_blur(d)
        down = down * (2.0 / 3.0)
        for q in range(3):
            x = xa[q, at8, :].reshape(BATCH, 8, 128)
            part = ua[3 + q][at8, :].reshape(BATCH, 8, 128)
            grad[pl.ds(at, BATCH), q * 8 : q * 8 + 8, :] = part + down * x
        return carry

    def segment(n, carry):
        lax.fori_loop(8 * n, 8 * n + 8, pair, 0)
        epilogue(4 + n, 0)
        finished(4 + n)
        return carry

    lax.fori_loop(0, 4, segment, 0)
    backward(jnp.int32(unit_count - 2), save[0])
    backward(jnp.int32(unit_count - 1), save[1])

    for group in range(n_own // 8):
        for s in range(8):
            rows = pl.ds(group * 64 + s, 8, stride=8)
            for k in range(6):
                ua[k][rows, :] = ub[k][s, group * 8 : group * 8 + 8, :]

    def last(step, carry):
        epilogue(step, 0)
        finished(step)
        return carry

    lax.fori_loop(0, 4, last, 0)
    last(8, 0)

    @pl.when(more)
    def _():
        lax.fori_loop(9, TABLE // BATCH, last, 0)


def lane_order(flip):
    a = lax.broadcasted_iota(jnp.int32, (128, 128), 1 if flip else 0)
    b = lax.broadcasted_iota(jnp.int32, (128, 128), 0 if flip else 1)
    to = ((a >> 5) * 2 + (a & 1)) * 16 + ((a >> 1) & 15)
    return jnp.where(to == b, 1.0, 0.0)


def swap_groups(rows):
    group = lax.broadcasted_iota(jnp.int32, rows[0].shape, 1) >> 4
    out = []
    for s in range(8):
        total = rows[s]
        for j in range(8):
            if j != s:
                total = jnp.where(group == j, pltpu.roll(rows[j], (j - s) * 16 % 128, 1), total)
        out.append(total)
    return out


def to_rows(images, spread, mine):
    order = lane_order(False).astype(jnp.bfloat16)
    for ch in range(3):
        tall = jnp.concatenate(
            [images[:, (ch * 8 + j) * 128 : (ch * 8 + j + 1) * 128].astype(jnp.float32) for j in range(8)]
        )
        tall = jnp.dot(tall.astype(jnp.bfloat16), order, preferred_element_type=jnp.float32)
        rows = swap_groups([tall[4 * j : 4 * j + 4] for j in range(8)])
        for s in range(8):
            spread[pl.ds(ch * 8 + s, 4, stride=24), :] = rows[s]
    for k in range(4):
        mine[k] = spread[24 * k : 24 * k + 24, :].astype(jnp.bfloat16)


def from_rows(spread, out):
    order = lane_order(True)
    for ch in range(3):
        rows = swap_groups([spread[pl.ds(ch * 8 + s, 4, stride=24), :] for s in range(8)])
        tall = jnp.dot(
            jnp.concatenate(rows), order, precision=lax.Precision.HIGHEST, preferred_element_type=jnp.float32
        )
        for j in range(8):
            out[:, (ch * 8 + j) * 128 : (ch * 8 + j + 1) * 128] = tall[4 * j : 4 * j + 4]


ROWS = 16
COLS = 8
EXTRA = 18
SLOTS = 32 + EXTRA
TABLE = 88
TILES = 6
MESH = pl.DeviceIdType.MESH


def place():
    return lax.axis_index("row"), lax.axis_index("col")


def greet(r, c):
    barrier = pltpu.get_barrier_semaphore()
    x, y, z = (r >> 1) & 3, c >> 1, ((c & 1) << 1) + (r >> 3)
    xs = [((x + d) & 3) << 1 for d in range(4)]
    ys = [((y + d) & 3) << 1 for d in range(4)]
    zs = [((z + d) & 3) for d in range(4)]
    cores = [r & 1, 1 - (r & 1)]
    far = lambda o: sum(min(d, 4 - d) for d in o[:3]) + 0.1 * o[3]
    steps = [(i, j, k, l) for i in range(4) for j in range(4) for k in range(4) for l in range(2)]
    for i, j, k, l in sorted(steps, key=far, reverse=True)[:-1]:
        rr = ((zs[k] & 1) << 3) + xs[i] + cores[l]
        pl.semaphore_signal(barrier, inc=1, device_id=(rr, ys[j] + (zs[k] >> 1)), device_id_type=MESH)


def enter():
    pl.semaphore_wait(pltpu.get_barrier_semaphore(), ROWS * COLS - 1)


def ship(go, away, rr, cc, src, dst, send_sem, recv_sem):
    def remote():
        pltpu.make_async_remote_copy(src, dst, send_sem, recv_sem, device_id=(rr, cc), device_id_type=MESH).start()

    def local():
        pltpu.make_async_copy(src, dst, recv_sem).start()

    guarded(go, away, remote)
    if away is not None:
        guarded(go, jnp.logical_not(away), local)


def shipped(go, away, rr, cc, src, dst, send_sem, recv_sem):
    guarded(go, away, lambda: pltpu.make_async_copy(src, src, send_sem).wait())


def guarded(one, two, work):
    conds = [x for x in (one, two) if x is not None]
    if not conds:
        work()
        return
    cond = conds[0] if len(conds) == 1 else jnp.logical_and(*conds)

    @pl.when(cond)
    def _():
        work()


def arrived(dst, recv_sem):
    pltpu.make_async_copy(dst, dst, recv_sem).wait()


def image_routes(r, c):
    e = ((c & 1) << 4) + r
    early = e < 16
    for k in range(4):
        block = 4 * k + (c >> 1)
        for i in range(COLS):
            d = (c + i) & 7
            yield k, block, d, e, (block != r if i == 0 else None)
            rr = (block + 16 - d) & 15
            yield k, rr, d, 32 + e, (rr != r if i == 0 else None)
        rr = (block + 8) & 15
        d = jnp.where(early, e >> 1, 0)
        slot = jnp.where(early, 64 + (e & 1), 50 + e)
        yield k, rr, d, slot, jnp.logical_or(rr != r, d != c)


def slot_count_of(c):
    return jnp.where(c == 0, 32 + EXTRA, 34)


def cot_route(r, c, h, k):
    q = c & 1
    block = 4 * k + (c >> 1)
    dd = block - r
    straight = jnp.logical_or(dd < 8, jnp.logical_and(dd == 8, q == h))
    single = jnp.logical_and(dd >= 0, dd != 8)
    if h == 1:
        single = jnp.logical_and(single, jnp.logical_or(dd != 0, q == 1))
    near = dd < 8
    rr = jnp.where(near, r, block)
    cc = jnp.where(near, dd, 16 - dd) & 7
    slot = jnp.where(near, h * 2 + q, q * 2 + h)
    return dd, single, straight, rr, cc, slot


def tangents(op, r, c, cots, tiles, cot_send, cot_recv, far_send):
    for h in range(2):
        for k in range(4):
            idx = h * 4 + k
            dd, single, straight, rr, cc, slot = cot_route(r, c, h, k)
            src = cots.at[idx]
            op(single, dd != c, rr, cc, src, tiles.at[slot], cot_send.at[idx], cot_recv.at[slot])

            @pl.when(dd == 8)
            def _():
                row = jnp.where(straight, r, (r + 8) & 15)
                for i in range(COLS if h == 0 else 1):
                    d = (c + i) & 7 if h == 0 else 0
                    away = jnp.logical_not(straight) if i == 0 else None
                    if h == 1:
                        away = jnp.logical_or(away, c != 0)
                    op(None, away, row, d, src, tiles.at[4 + h], far_send.at[h * 8 + i], cot_recv.at[4 + h])


def partial_route(r, c, batch, n):
    slot = batch * BATCH + n
    main = batch < 8
    own = batch < 4
    x = slot - 64
    e = jnp.where(main, slot & 31, jnp.where(x < 2, 2 * c + x, 14 + x))
    block = jnp.where(own, r, jnp.where(main, r + c, r + 8) & 15)
    j = 2 * block + (e >> 4)
    source = jnp.where(own, c, jnp.where(main, 8 + c, 16))
    return slot, e & 15, j & 7, j >> 3, source


def tile_route(r, c, slot):
    far = slot >= 4
    bb, qa = slot // 2, slot % 2
    other = (r + 8) & 15 if far else (r + c) & 15
    if far:
        bb = jnp.where(r < 8, qa, 1 - qa)
    ahead = other >= r
    i = jnp.where(ahead, 2 * r + bb, 2 * other + qa)
    j = jnp.where(ahead, 2 * other + qa, 2 * r + bb)
    return i >> 1, j & 7, i & 1, j >> 3


def whole_kernel(images_in, cot_in, images_out, kernel_ref, mine, cots, spread, cot32, kernel_out, *rest):
    table, tiles, grads, kouts, parts, far = rest[:6]
    img_send, img_recv, cot_send, cot_recv, far_send = rest[6:11]
    part_send, part_recv, tile_send, tile_recv, far_recv = rest[11:16]
    r, c = place()
    greet(r, c)
    to_rows(images_in, spread, mine)
    cot32[...] = jnp.zeros_like(cot32)
    for h in range(2):
        for row in range(16):
            part = cot_in[h, row].astype(jnp.float32)
            cot32[pl.ds(h * 64 + row, 4, stride=16), 0:16] = part
    for idx in range(8):
        cots[idx] = cot32[16 * idx : 16 * idx + 16, :].astype(jnp.bfloat16)
    enter()

    def images(op):
        for idx, (k, rr, cc, slot, away) in enumerate(image_routes(r, c)):
            op(None, away, rr, cc, mine.at[k], table.at[slot], img_send.at[idx], img_recv.at[slot])

    images(ship)
    tangents(ship, r, c, cots, tiles, cot_send, cot_recv, far_send)
    for slot in (0, 1, 3, 4):
        arrived(tiles.at[slot], cot_recv.at[slot])

    @pl.when(c != 0)
    def _():
        arrived(tiles.at[2], cot_recv.at[2])
        tiles[5] = jnp.zeros((16, 128), jnp.bfloat16)
        for slot in range(66, 72):
            table[slot] = jnp.zeros((24, 128), jnp.bfloat16)

    @pl.when(c == 0)
    def _():
        arrived(tiles.at[5], cot_recv.at[5])
        tiles[2] = jnp.zeros((16, 128), jnp.bfloat16)
        for slot in range(32 + SLOTS, TABLE):
            table[slot] = jnp.zeros((24, 128), jnp.bfloat16)

    def used(batch, n):
        slot = batch * BATCH + n
        return jnp.logical_or(slot < 66, jnp.logical_and(c == 0, slot < 32 + SLOTS))

    def landed(batch):
        for n in range(BATCH):
            slot = batch * BATCH + n
            guarded(used(batch, n), None, lambda: arrived(table.at[slot], img_recv.at[slot]))

    def partials(op, batch):
        for n in range(BATCH):
            slot, rr, cc, k, source = partial_route(r, c, batch, n)
            away = jnp.logical_or(rr != r, cc != c)
            op(used(batch, n), away, rr, cc, grads.at[slot], parts.at[k, source], part_send.at[slot], part_recv.at[k, source])

    for slot in range(TILES):
        cot32[16 * slot : 16 * slot + 16, :] = tiles[slot].astype(jnp.float32)

    compute_kernel(
        32, plan, landed, lambda batch: partials(ship, batch), table, cot32, kouts, grads, *rest[16:]
    )

    def outputs(op):
        for slot in range(TILES):
            rr, cc, h, k = tile_route(r, c, slot)
            go = (None, None, c != 0, None, None, c == 0)[slot]
            if slot == 4:
                dst, sem = far.at[c], far_recv.at[c]
            else:
                dst, sem = kernel_out.at[pl.ds(pl.multiple_of((h * 4 + k) * 16, 16), 16)], tile_recv.at[h * 4 + k]
            away = jnp.logical_or(rr != r, cc != c)
            op(go, away, rr, cc, kouts.at[slot], dst, tile_send.at[slot], sem)

    outputs(ship)

    for h in range(2):
        for k in range(4):
            dd, single, straight, rr, cc, slot = cot_route(r, c, h, k)
            spot = h * 4 + k
            if h == 0:

                @pl.when(dd == 8)
                def _():
                    for d in range(COLS):
                        arrived(far.at[d], far_recv.at[d])
                    total = far[0]
                    for d in range(1, COLS):
                        total = total + far[d]
                    kernel_out[16 * spot : 16 * spot + 16, :] = total

                get = single
            else:
                get = jnp.logical_or(single, dd == 8)

            @pl.when(get)
            def _():
                arrived(kernel_out.at[16 * spot : 16 * spot + 16], tile_recv.at[spot])

            unused = dd < 0
            if h == 1:
                unused = jnp.logical_or(unused, jnp.logical_and(dd == 0, (c & 1) == 0))

            @pl.when(unused)
            def _():
                kernel_out[16 * spot : 16 * spot + 16, :] = jnp.zeros((16, 128), jnp.float32)

    for k in range(4):
        for source in range(17):
            arrived(parts.at[k, source], part_recv.at[k, source])
        total = parts[k, 0]
        for source in range(1, 17):
            total = total + parts[k, source]
        spread[24 * k : 24 * k + 24, :] = total

    from_rows(spread, images_out)
    for h in range(2):
        for row in range(16):
            kernel_ref[h, row] = kernel_out[pl.ds(h * 64 + row, 4, stride=16), :][:, 0:16]
    images(shipped)
    tangents(shipped, r, c, cots, tiles, cot_send, cot_recv, far_send)
    outputs(shipped)

    def settle(batch, carry):
        partials(shipped, batch)
        return carry

    lax.fori_loop(0, TABLE // BATCH, settle, 0)


def whole_call(mine, cots):
    whole = pl.BlockSpec(memory_space=pltpu.VMEM)
    dma = pltpu.SemaphoreType.DMA
    vm = lambda *shape: pltpu.VMEM(shape, jnp.float32)
    own, rows = 32, TABLE * 8
    return pl.pallas_call(
        whole_kernel,
        out_shape=(
            jax.ShapeDtypeStruct((4, 3072), jnp.float32),
            jax.ShapeDtypeStruct((2, 16, 4, 16), jnp.float32),
        ),
        in_specs=[whole, whole],
        out_specs=(whole, whole),
        scratch_shapes=[
            pltpu.VMEM((4, 24, 128), jnp.bfloat16),
            pltpu.VMEM((8, 16, 128), jnp.bfloat16),
            vm(96, 128),
            vm(128, 128),
            vm(128, 128),
            pltpu.VMEM((TABLE, 24, 128), jnp.bfloat16),
            pltpu.VMEM((TILES, 16, 128), jnp.bfloat16),
            vm(TABLE, 24, 128),
            vm(TILES, 16, 128),
            vm(4, 17, 24, 128),
            vm(8, 16, 128),
        ]
        + [dma((68,)), dma((32 + SLOTS,)), dma((8,)), dma((TILES,)), dma((16,))]
        + [dma((32 + SLOTS,)), dma((4, 17)), dma((TILES,)), dma((8,)), dma((8,))]
        + [vm(3, rows, 128)] * 3
        + [vm(3, 8, own, 128)] * 3
        + [vm(8, own, 128)] * 6
        + [vm(rows, 128)] * 6
        + ([vm(8, 16, 128)] * 5 + [vm(64, 128)] * 6) * 2,
        compiler_params=pltpu.CompilerParams(
            collective_id=0, has_side_effects=True, vmem_limit_bytes=56 * 1024 * 1024
        ),
    )(mine, cots)


def plan():
    r, c = place()

    def unit_of(u):
        first = c == 0
        n = u - jnp.where(first, 48, 64)
        main = n < 0
        e = jnp.where(n < 2, 2 * c + n, 14 + n)
        half = jnp.where(r < 8, e // 16, 1 - e // 16)
        short = jnp.logical_and(first, u < 16)
        v = jnp.where(first, u + 16, u)
        slot = jnp.where(main, jnp.where(short, u, v // 2), 32 + n)
        bb = jnp.where(main, jnp.where(short, 0, v % 2), half)
        tile = jnp.where(main, bb * 2 + slot // 16, 4 + e // 16)
        return slot, bb, tile, jnp.where(main, slot, e) % 16

    def turned(u):
        return jnp.where(u < jnp.where(c == 0, 48, 64), r + c >= ROWS, r >= 8)

    return 66, slot_count_of(c), unit_of, turned


def body(images, cotangent):
    image_grads, kernel = whole_call(images.reshape(4, 3072), cotangent.reshape(2, 16, 4, 16))
    return kernel.reshape(2, 16, 4, 1, 16), image_grads.reshape(4, 1, 1, 3072)


def solution(mesh):
    return jax.shard_map(
        body,
        mesh=mesh,
        in_specs=(P(None, "col", "row", None), P("row", None, None, "col", None)),
        out_specs=(P("row", None, None, "col", None), P(None, "col", "row", None)),
        check_vma=False,
    )
```

```python
import math

import jax
import jax.numpy as jnp
from jax import lax
from jax.experimental import pallas as pl
from jax.experimental.pallas import tpu as pltpu
from jax.sharding import PartitionSpec as P

WEIGHT_VAR = 2.0
BIAS_VAR = 0.1
LAYERS = 3
ALPHA = [WEIGHT_VAR / 27.0]
for _ in range(LAYERS - 1):
    ALPHA.append(ALPHA[-1] * WEIGHT_VAR / 9.0)
BIAS = [BIAS_VAR / a for a in ALPHA]
ASIN = [
    a / (2.0 * math.pi)
    for a in (
        -0.10520251251688581,
        1.0690300997862225,
        0.9916991797412131,
        -0.4865441702586394,
        0.1018140487237715,
    )
]
TINY = 1e-30
BATCH = 8
HALVES = 2


def lane_masks(shape):
    lane = lax.broadcasted_iota(jnp.int32, shape, len(shape) - 1)
    f = jnp.float32
    return (
        (lane % 16 != 0).astype(f),
        (lane % 16 != 15).astype(f),
        (lane >= 16).astype(f),
        (lane < 112).astype(f),
    )


def compute_kernel(n_own, plan, landed, finished, tiled, img, cot, kout, grad, xa, ra, ta, xb, rb, tb, *rest):
    ub, ua, save = rest[:6], rest[6:12], (rest[12:23], rest[23:34])
    f32 = jnp.float32
    unit_count, slot_count, unit_of, turned = plan()
    left, right, upper, lower = lane_masks((16, 128))

    row3 = lax.broadcasted_iota(jnp.int32, (BATCH, 8, 128), 1)
    masks3 = lane_masks((BATCH, 8, 128))

    def image_blur(v):
        even = row3 % 2 == 0
        mate = jnp.where(even, pltpu.roll(v, 7, 1), pltpu.roll(v, 1, 1))
        side = jnp.where(even, masks3[0] * pltpu.roll(mate, 1, 2), masks3[1] * pltpu.roll(mate, 127, 2))
        h = v + mate + side
        above = pltpu.roll(h, 2, 1)
        below = pltpu.roll(h, 6, 1)
        above = jnp.where(row3 < 2, masks3[2] * pltpu.roll(above, 16, 2), above)
        below = jnp.where(row3 >= 6, masks3[3] * pltpu.roll(below, 112, 2), below)
        return h + above + below

    def prologue(step, carry):
        at = pl.multiple_of(step * BATCH, BATCH)
        at8 = pl.ds(pl.multiple_of(step * BATCH * 8, BATCH * 8), BATCH * 8)
        val = img[pl.ds(at, BATCH)].astype(f32)
        var = jnp.zeros((BATCH, 8, 128), f32)
        for ch in range(3):
            x = val[:, ch * 8 : ch * 8 + 8, :]
            xa[ch, at8, :] = x.reshape(BATCH * 8, 128)
            var = var + x * x
        var = var * (1.0 / 3.0)
        for layer in range(LAYERS):
            area = (WEIGHT_VAR / 9.0) * image_blur(var) + BIAS_VAR
            inv = lax.rsqrt(area)
            ra[layer, at8, :] = (inv * math.sqrt(ALPHA[layer])).reshape(BATCH * 8, 128)
            ta[layer, at8, :] = (
                area * inv * (1.0 / math.sqrt(2.0 * math.pi * ALPHA[layer]))
            ).reshape(BATCH * 8, 128)
            var = 0.5 * area
        for k in range(6):
            ua[k][at8, :] = jnp.zeros((BATCH * 8, 128), f32)
        return carry

    more = slot_count > 34

    def fetched(step, carry):
        landed(step)
        return prologue(step, carry)

    lax.fori_loop(0, 4, fetched, 0)
    lax.fori_loop(8, jnp.where(more, TABLE // BATCH, 9), fetched, 0)
    fetched(4, 0)

    for group in range(n_own // 8):
        for s in range(8):
            rows = pl.ds(group * 64 + s, 8, stride=8)
            part = slice(group * 8, group * 8 + 8)
            for q in range(3):
                xb[q, s, part, :] = xa[q, rows, :]
                rb[q, s, part, :] = ra[q, rows, :]
                tb[q, s, part, :] = ta[q, rows, :]
    for k in range(6):
        ub[k][...] = jnp.zeros_like(ub[k])
    kout[...] = jnp.zeros_like(kout)

    def across(v):
        out = [None] * 8
        for p in range(0, 8, 2):
            mid = v[p] + v[p + 1]
            out[p] = mid + left * pltpu.roll(v[p + 1], 1, 1)
            out[p + 1] = mid + right * pltpu.roll(v[p], 127, 1)
        return out

    def vertical(h, bias):
        w = [None] * 8
        for sx in range(2):
            top = upper * pltpu.roll(h[6 + sx], 16, 1)
            bottom = lower * pltpu.roll(h[sx], 112, 1)
            one = h[sx] + h[2 + sx]
            two = h[4 + sx] + h[6 + sx]
            if bias is not None:
                one = one + bias
                two = two + bias
            w[sx] = one + top
            w[2 + sx] = one + h[4 + sx]
            w[4 + sx] = h[2 + sx] + two
            w[6 + sx] = two + bottom
        return w

    lane16 = lax.broadcasted_iota(jnp.int32, (16, 128), 1)
    row16 = lax.broadcasted_iota(jnp.int32, (16, 128), 0)
    ORDER = (0, 7, 1, 6, 2, 5, 3, 4)

    def ready(u):
        slot, bb, tile, lane = unit_of(u)
        base = pl.multiple_of((n_own + slot) * 8, 8)
        own = pl.ds(pl.multiple_of(bb * 16, 16), 16)
        return base, own, tile, lane

    def arow(ref, q, base, s):
        return ref[q, pl.ds(base + s, 1), :]

    def fold(uacc, k, base):
        total = uacc[k][pl.ds(0, 8, stride=8), :]
        for b in range(1, 8):
            total = total + uacc[k][pl.ds(b, 8, stride=8), :]
        ua[k][pl.ds(base, 8), :] += total

    def tally(uacc, k, s, own, e_own, e_slot):
        ub[k][s, own, :] += e_own
        uacc[k][s * 8 : s * 8 + 8, :] = e_slot[:8] + e_slot[8:]

    def forward(u, saved):
        sg1, sz1, sg2, sz2, sh, *uacc = saved
        base, own, tile, lane = ready(u)
        h = [None] * 8
        for s in ORDER:
            x = xb[0, s, own, :] * arow(xa, 0, base, s)
            x = x + xb[1, s, own, :] * arow(xa, 1, base, s)
            x = x + xb[2, s, own, :] * arow(xa, 2, base, s)
            h[s] = x
        h = across(h)
        spin = turned(u)
        row = cot[pl.ds(tile * 16 + lane, 1), :]
        source = jnp.where(spin, jnp.broadcast_to(row, (16, 128)), cot[pl.ds(pl.multiple_of(tile * 16, 16), 16), :])
        weight = jnp.where(lane16 == jnp.where(spin, row16, lane), source, 0.0)
        weight = jnp.sum(weight, axis=1, keepdims=True) * (WEIGHT_VAR * ALPHA[2] / 1024.0)
        weight = jnp.broadcast_to(weight, (16, 128))
        total = None
        for layer in range(LAYERS):
            w = vertical(h, BIAS[layer])
            h = [None] * 8
            for s in ORDER:
                c = (w[s] * rb[layer, s, own, :]) * arow(ra, layer, base, s)
                y = jnp.maximum(1.0 - c * c, TINY)
                sine = y * lax.rsqrt(y)
                v = lax.rsqrt(1.0 + sine)
                poly = ASIN[4] * v + ASIN[3]
                for k in range(2, -1, -1):
                    poly = poly * v + ASIN[k]
                g = c * poly + 0.25
                z = (sine * tb[layer, s, own, :]) * arow(ta, layer, base, s)
                f = w[s] * g + z
                if layer < LAYERS - 1:
                    (sg1, sg2)[layer][s] = g
                    (sz1, sz2)[layer][s] = z
                    h[s] = f
                else:
                    total = f if total is None else total + f
                    e = weight * z
                    tally(uacc, layer, s, own, e, e)
                    h[s] = weight * g
            h = across(h)
        for s in range(8):
            sh[s] = h[s]
        fold(uacc, LAYERS - 1, base)
        value = jnp.sum(total, axis=1, keepdims=True) * (WEIGHT_VAR * ALPHA[2] / 1024.0) + BIAS_VAR
        value = jnp.broadcast_to(value, (16, 128))
        flat = jnp.sum(jnp.where(lane16 == row16, value, 0.0), axis=0, keepdims=True)
        value = jnp.where(spin, jnp.broadcast_to(flat, (16, 128)), value)
        kout[tile] = jnp.where(jnp.where(spin, row16, lane16) == lane, value, kout[tile])

    def backward(u, saved):
        sg1, sz1, sg2, sz2, sh, *uacc = saved
        base, own, tile, lane = ready(u)
        h = [sh[s] for s in range(8)]
        for layer in range(LAYERS - 2, -1, -1):
            w = vertical(h, None)
            h = [None] * 8
            for s in ORDER:
                e = w[s] * (sz1, sz2)[layer][s]
                tally(uacc, layer, s, own, e, e)
                h[s] = w[s] * (sg1, sg2)[layer][s]
            h = across(h)
            fold(uacc, layer, base)
        w = vertical(h, None)
        for s in range(8):
            for q in range(3):
                tally(uacc, 3 + q, s, own, w[s] * arow(xa, q, base, s), w[s] * xb[q, s, own, :])
        for q in range(3):
            fold(uacc, 3 + q, base)

    forward(jnp.int32(0), save[0])
    forward(jnp.int32(1), save[1])

    def gather_own(block):
        for group in (2 * block, 2 * block + 1):
            for s in range(8):
                rows = pl.ds(group * 64 + s, 8, stride=8)
                for k in range(6):
                    ua[k][rows, :] = ub[k][s, group * 8 : group * 8 + 8, :]

    def pairs(j, carry):
        @pl.when(jnp.logical_or(j == 2, jnp.logical_or(j == 4, j == 6)))
        def _():
            fetched(4 + (j >> 1), 0)

        for n in range(2):
            u = 4 * j + 2 * n
            backward(u, save[0])
            forward(u + 2, save[0])
            backward(u + 1, save[1])
            forward(u + 3, save[1])

        @pl.when(jnp.logical_or(j == 4, jnp.logical_or(j == 10, jnp.logical_or(j == 12, j == 14))))
        def _():
            low = jnp.where(j == 4, 8, (j >> 1) - 1)
            high = jnp.where(jnp.logical_and(j == 4, more), TABLE // BATCH, low + 1)
            lax.fori_loop(low, high, last, 0)

        @pl.when(j == 12)
        def _():
            gather_own(0)
            lax.fori_loop(0, 2, last, 0)

        return carry

    def epilogue(step, carry):
        at = pl.multiple_of(step * BATCH, BATCH)
        at8 = pl.ds(pl.multiple_of(step * BATCH * 8, BATCH * 8), BATCH * 8)
        down = None
        for layer in range(LAYERS - 1, -1, -1):
            r = ra[layer, at8, :]
            d = ua[layer][at8, :] * (r * r) * (0.5 / ALPHA[layer])
            d = d.reshape(BATCH, 8, 128)
            if down is not None:
                d = d + 0.5 * down
            down = (WEIGHT_VAR / 9.0) * image_blur(d)
        down = down * (2.0 / 3.0)
        for q in range(3):
            x = xa[q, at8, :].reshape(BATCH, 8, 128)
            part = ua[3 + q][at8, :].reshape(BATCH, 8, 128)
            grad[pl.ds(at, BATCH), q * 8 : q * 8 + 8, :] = part + down * x
        return carry

    def last(step, carry):
        epilogue(step, 0)
        finished(step)
        return carry

    lax.fori_loop(0, (unit_count - 2) // 4, pairs, 0)
    tiled()
    backward(jnp.int32(unit_count - 2), save[0])
    backward(jnp.int32(unit_count - 1), save[1])
    gather_own(1)
    lax.fori_loop(2, 4, last, 0)
    last(7, 0)


def lane_order(flip):
    a = lax.broadcasted_iota(jnp.int32, (128, 128), 1 if flip else 0)
    b = lax.broadcasted_iota(jnp.int32, (128, 128), 0 if flip else 1)
    to = ((a >> 5) * 2 + (a & 1)) * 16 + ((a >> 1) & 15)
    return jnp.where(to == b, 1.0, 0.0)


def swap_groups(rows):
    group = lax.broadcasted_iota(jnp.int32, rows[0].shape, 1) >> 4
    out = []
    for s in range(8):
        total = rows[s]
        for j in range(8):
            if j != s:
                total = jnp.where(group == j, pltpu.roll(rows[j], (j - s) * 16 % 128, 1), total)
        out.append(total)
    return out


def to_rows(images, spread, mine):
    order = lane_order(False).astype(jnp.bfloat16)
    for ch in range(3):
        tall = jnp.concatenate(
            [images[:, (ch * 8 + j) * 128 : (ch * 8 + j + 1) * 128].astype(jnp.float32) for j in range(8)]
        )
        tall = jnp.dot(tall.astype(jnp.bfloat16), order, preferred_element_type=jnp.float32)
        rows = swap_groups([tall[4 * j : 4 * j + 4] for j in range(8)])
        for s in range(8):
            spread[pl.ds(ch * 8 + s, 4, stride=24), :] = rows[s]
    for k in range(4):
        mine[k] = spread[24 * k : 24 * k + 24, :].astype(jnp.bfloat16)


def from_rows(spread, out):
    order = lane_order(True)
    for ch in range(3):
        rows = swap_groups([spread[pl.ds(ch * 8 + s, 4, stride=24), :] for s in range(8)])
        tall = jnp.dot(
            jnp.concatenate(rows), order, precision=lax.Precision.HIGHEST, preferred_element_type=jnp.float32
        )
        for j in range(8):
            out[:, (ch * 8 + j) * 128 : (ch * 8 + j + 1) * 128] = tall[4 * j : 4 * j + 4]


ROWS = 16
COLS = 8
EXTRA = 18
SLOTS = 32 + EXTRA
TABLE = 88
TILES = 6
MESH = pl.DeviceIdType.MESH


def place():
    return lax.axis_index("row"), lax.axis_index("col")


def greet(r, c):
    barrier = pltpu.get_barrier_semaphore()
    x, y, z = (r >> 1) & 3, c >> 1, ((c & 1) << 1) + (r >> 3)
    xs = [((x + d) & 3) << 1 for d in range(4)]
    ys = [((y + d) & 3) << 1 for d in range(4)]
    zs = [((z + d) & 3) for d in range(4)]
    cores = [r & 1, 1 - (r & 1)]
    far = lambda o: sum(min(d, 4 - d) for d in o[:3]) + 0.1 * o[3]
    steps = [(i, j, k, l) for i in range(4) for j in range(4) for k in range(4) for l in range(2)]
    for i, j, k, l in sorted(steps, key=far, reverse=True)[:-1]:
        rr = ((zs[k] & 1) << 3) + xs[i] + cores[l]
        pl.semaphore_signal(barrier, inc=1, device_id=(rr, ys[j] + (zs[k] >> 1)), device_id_type=MESH)


def enter():
    pl.semaphore_wait(pltpu.get_barrier_semaphore(), ROWS * COLS - 1)


def ship(go, away, rr, cc, src, dst, send_sem, recv_sem):
    def remote():
        pltpu.make_async_remote_copy(src, dst, send_sem, recv_sem, device_id=(rr, cc), device_id_type=MESH).start()

    def local():
        pltpu.make_async_copy(src, dst, recv_sem).start()

    guarded(go, away, remote)
    if away is not None:
        guarded(go, jnp.logical_not(away), local)


def shipped(go, away, rr, cc, src, dst, send_sem, recv_sem):
    guarded(go, away, lambda: pltpu.make_async_copy(src, src, send_sem).wait())


def guarded(one, two, work):
    conds = [x for x in (one, two) if x is not None]
    if not conds:
        work()
        return
    cond = conds[0] if len(conds) == 1 else jnp.logical_and(*conds)

    @pl.when(cond)
    def _():
        work()


def arrived(dst, recv_sem):
    pltpu.make_async_copy(dst, dst, recv_sem).wait()


def image_routes(r, c):
    e = ((c & 1) << 4) + r
    early = e < 16
    for k in range(4):
        block = 4 * k + (c >> 1)
        for i in range(COLS):
            d = (c + i) & 7
            yield k, block, d, e, (block != r if i == 0 else None)
            rr = (block + 16 - d) & 15
            yield k, rr, d, 32 + e, (rr != r if i == 0 else None)
        rr = (block + 8) & 15
        d = jnp.where(early, e >> 1, 0)
        slot = jnp.where(early, 64 + (e & 1), 50 + e)
        yield k, rr, d, slot, jnp.logical_or(rr != r, d != c)


def slot_count_of(c):
    return jnp.where(c == 0, 32 + EXTRA, 34)


def cot_route(r, c, h, k):
    q = c & 1
    block = 4 * k + (c >> 1)
    dd = block - r
    straight = jnp.logical_or(dd < 8, jnp.logical_and(dd == 8, q == h))
    single = jnp.logical_and(dd >= 0, dd != 8)
    if h == 1:
        single = jnp.logical_and(single, jnp.logical_or(dd != 0, q == 1))
    near = dd < 8
    rr = jnp.where(near, r, block)
    cc = jnp.where(near, dd, 16 - dd) & 7
    slot = jnp.where(near, h * 2 + q, q * 2 + h)
    return dd, single, straight, rr, cc, slot


def tangents(op, r, c, cots, tiles, cot_send, cot_recv, far_send):
    for h in range(2):
        for k in range(4):
            idx = h * 4 + k
            dd, single, straight, rr, cc, slot = cot_route(r, c, h, k)
            src = cots.at[idx]
            op(single, dd != c, rr, cc, src, tiles.at[slot], cot_send.at[idx], cot_recv.at[slot])

            @pl.when(dd == 8)
            def _():
                row = jnp.where(straight, r, (r + 8) & 15)
                for i in range(COLS if h == 0 else 1):
                    d = (c + i) & 7 if h == 0 else 0
                    away = jnp.logical_not(straight) if i == 0 else None
                    if h == 1:
                        away = jnp.logical_or(away, c != 0)
                    op(None, away, row, d, src, tiles.at[4 + h], far_send.at[h * 8 + i], cot_recv.at[4 + h])


def partial_route(r, c, batch, n):
    slot = batch * BATCH + n
    main = batch < 8
    own = batch < 4
    x = slot - 64
    e = jnp.where(main, slot & 31, jnp.where(x < 2, 2 * c + x, 14 + x))
    block = jnp.where(own, r, jnp.where(main, r + c, r + 8) & 15)
    j = 2 * block + (e >> 4)
    source = jnp.where(own, c, jnp.where(main, 8 + c, 16))
    return slot, e & 15, j & 7, j >> 3, source


def tile_route(r, c, slot):
    far = slot >= 4
    bb, qa = slot // 2, slot % 2
    other = (r + 8) & 15 if far else (r + c) & 15
    if far:
        bb = jnp.where(r < 8, qa, 1 - qa)
    ahead = other >= r
    i = jnp.where(ahead, 2 * r + bb, 2 * other + qa)
    j = jnp.where(ahead, 2 * other + qa, 2 * r + bb)
    return i >> 1, j & 7, i & 1, j >> 3


def whole_kernel(images_in, cot_in, images_out, kernel_ref, mine, cots, spread, cot32, kernel_out, *rest):
    table, tiles, grads, kouts, parts, far = rest[:6]
    img_send, img_recv, cot_send, cot_recv, far_send = rest[6:11]
    part_send, part_recv, tile_send, tile_recv, far_recv = rest[11:16]
    r, c = place()
    greet(r, c)
    to_rows(images_in, spread, mine)
    cot32[...] = jnp.zeros_like(cot32)
    for h in range(2):
        for row in range(16):
            part = cot_in[h, row].astype(jnp.float32)
            cot32[pl.ds(h * 64 + row, 4, stride=16), 0:16] = part
    for idx in range(8):
        cots[idx] = cot32[16 * idx : 16 * idx + 16, :].astype(jnp.bfloat16)
    enter()

    def images(op):
        for idx, (k, rr, cc, slot, away) in enumerate(image_routes(r, c)):
            op(None, away, rr, cc, mine.at[k], table.at[slot], img_send.at[idx], img_recv.at[slot])

    images(ship)
    tangents(ship, r, c, cots, tiles, cot_send, cot_recv, far_send)
    for slot in (0, 1, 3, 4):
        arrived(tiles.at[slot], cot_recv.at[slot])

    @pl.when(c != 0)
    def _():
        arrived(tiles.at[2], cot_recv.at[2])
        tiles[5] = jnp.zeros((16, 128), jnp.bfloat16)
        for slot in range(66, 72):
            table[slot] = jnp.zeros((24, 128), jnp.bfloat16)

    @pl.when(c == 0)
    def _():
        arrived(tiles.at[5], cot_recv.at[5])
        tiles[2] = jnp.zeros((16, 128), jnp.bfloat16)
        for slot in range(32 + SLOTS, TABLE):
            table[slot] = jnp.zeros((24, 128), jnp.bfloat16)

    def used(batch, n):
        slot = batch * BATCH + n
        return jnp.logical_or(slot < 66, jnp.logical_and(c == 0, slot < 32 + SLOTS))

    def landed(batch):
        for n in range(BATCH):
            slot = batch * BATCH + n
            guarded(used(batch, n), None, lambda: arrived(table.at[slot], img_recv.at[slot]))

    def partials(op, batch):
        for n in range(BATCH):
            slot, rr, cc, k, source = partial_route(r, c, batch, n)
            away = jnp.logical_or(rr != r, cc != c)
            op(used(batch, n), away, rr, cc, grads.at[slot], parts.at[k, source], part_send.at[slot], part_recv.at[k, source])

    def outputs(op):
        for slot in range(TILES):
            rr, cc, h, k = tile_route(r, c, slot)
            go = (None, None, c != 0, None, None, c == 0)[slot]
            if slot == 4:
                dst, sem = far.at[c], far_recv.at[c]
            else:
                dst, sem = kernel_out.at[pl.ds(pl.multiple_of((h * 4 + k) * 16, 16), 16)], tile_recv.at[h * 4 + k]
            away = jnp.logical_or(rr != r, cc != c)
            op(go, away, rr, cc, kouts.at[slot], dst, tile_send.at[slot], sem)

    for slot in range(TILES):
        cot32[16 * slot : 16 * slot + 16, :] = tiles[slot].astype(jnp.float32)

    compute_kernel(
        32, plan, landed, lambda batch: partials(ship, batch), lambda: outputs(ship), table, cot32, kouts, grads, *rest[16:]
    )


    for h in range(2):
        for k in range(4):
            dd, single, straight, rr, cc, slot = cot_route(r, c, h, k)
            spot = h * 4 + k
            if h == 0:

                @pl.when(dd == 8)
                def _():
                    for d in range(COLS):
                        arrived(far.at[d], far_recv.at[d])
                    total = far[0]
                    for d in range(1, COLS):
                        total = total + far[d]
                    kernel_out[16 * spot : 16 * spot + 16, :] = total

                get = single
            else:
                get = jnp.logical_or(single, dd == 8)

            @pl.when(get)
            def _():
                arrived(kernel_out.at[16 * spot : 16 * spot + 16], tile_recv.at[spot])

            unused = dd < 0
            if h == 1:
                unused = jnp.logical_or(unused, jnp.logical_and(dd == 0, (c & 1) == 0))

            @pl.when(unused)
            def _():
                kernel_out[16 * spot : 16 * spot + 16, :] = jnp.zeros((16, 128), jnp.float32)

    for k in range(4):
        for source in range(17):
            arrived(parts.at[k, source], part_recv.at[k, source])
        total = parts[k, 0]
        for source in range(1, 17):
            total = total + parts[k, source]
        spread[24 * k : 24 * k + 24, :] = total

    from_rows(spread, images_out)
    for h in range(2):
        for row in range(16):
            kernel_ref[h, row] = kernel_out[pl.ds(h * 64 + row, 4, stride=16), :][:, 0:16]
    images(shipped)
    tangents(shipped, r, c, cots, tiles, cot_send, cot_recv, far_send)
    outputs(shipped)

    def settle(batch, carry):
        partials(shipped, batch)
        return carry

    lax.fori_loop(0, TABLE // BATCH, settle, 0)


def whole_call(mine, cots):
    whole = pl.BlockSpec(memory_space=pltpu.VMEM)
    dma = pltpu.SemaphoreType.DMA
    vm = lambda *shape: pltpu.VMEM(shape, jnp.float32)
    own, rows = 32, TABLE * 8
    return pl.pallas_call(
        whole_kernel,
        out_shape=(
            jax.ShapeDtypeStruct((4, 3072), jnp.float32),
            jax.ShapeDtypeStruct((2, 16, 4, 16), jnp.float32),
        ),
        in_specs=[whole, whole],
        out_specs=(whole, whole),
        scratch_shapes=[
            pltpu.VMEM((4, 24, 128), jnp.bfloat16),
            pltpu.VMEM((8, 16, 128), jnp.bfloat16),
            vm(96, 128),
            vm(128, 128),
            vm(128, 128),
            pltpu.VMEM((TABLE, 24, 128), jnp.bfloat16),
            pltpu.VMEM((TILES, 16, 128), jnp.bfloat16),
            vm(TABLE, 24, 128),
            vm(TILES, 16, 128),
            vm(4, 17, 24, 128),
            vm(8, 16, 128),
        ]
        + [dma((68,)), dma((32 + SLOTS,)), dma((8,)), dma((TILES,)), dma((16,))]
        + [dma((32 + SLOTS,)), dma((4, 17)), dma((TILES,)), dma((8,)), dma((8,))]
        + [vm(3, rows, 128)] * 3
        + [vm(3, 8, own, 128)] * 3
        + [vm(8, own, 128)] * 6
        + [vm(rows, 128)] * 6
        + ([vm(8, 16, 128)] * 5 + [vm(64, 128)] * 6) * 2,
        compiler_params=pltpu.CompilerParams(
            collective_id=0, has_side_effects=True, vmem_limit_bytes=56 * 1024 * 1024
        ),
    )(mine, cots)


def plan():
    r, c = place()

    first = c == 0
    extras = jnp.where(first, EXTRA, 2)

    def unit_of(u):
        v = u - extras
        main = v >= 0
        e = jnp.where(u < 2, 2 * c + u, 14 + u)
        half = jnp.where(r < 8, e >> 4, 1 - (e >> 4))
        early = v < 32
        slot = jnp.where(main, jnp.where(early, v, v - jnp.where(first, 16, 32)), 32 + u)
        bb = jnp.where(main, jnp.where(early, 0, 1), half)
        tile = jnp.where(main, bb * 2 + (slot >> 4), 4 + (e >> 4))
        return slot, bb, tile, jnp.where(main, slot, e) & 15

    def turned(u):
        return jnp.where(u < extras, r >= 8, r + c >= ROWS)

    return 66, slot_count_of(c), unit_of, turned


def body(images, cotangent):
    image_grads, kernel = whole_call(images.reshape(4, 3072), cotangent.reshape(2, 16, 4, 16))
    return kernel.reshape(2, 16, 4, 1, 16), image_grads.reshape(4, 1, 1, 3072)


def solution(mesh):
    return jax.shard_map(
        body,
        mesh=mesh,
        in_specs=(P(None, "col", "row", None), P("row", None, None, "col", None)),
        out_specs=(P("row", None, None, "col", None), P(None, "col", "row", None)),
        check_vma=False,
    )
```

```python
import math

import jax
import jax.numpy as jnp
from jax import lax
from jax.experimental import pallas as pl
from jax.experimental.pallas import tpu as pltpu
from jax.sharding import PartitionSpec as P

WEIGHT_VAR = 2.0
BIAS_VAR = 0.1
LAYERS = 3
ALPHA = [WEIGHT_VAR / 27.0]
for _ in range(LAYERS - 1):
    ALPHA.append(ALPHA[-1] * WEIGHT_VAR / 9.0)
BIAS = [BIAS_VAR / a for a in ALPHA]
ASIN = [
    a / (2.0 * math.pi)
    for a in (
        -0.10520251251688581,
        1.0690300997862225,
        0.9916991797412131,
        -0.4865441702586394,
        0.1018140487237715,
    )
]
TINY = 1e-30
BATCH = 8
HALVES = 2


def lane_masks(shape):
    lane = lax.broadcasted_iota(jnp.int32, shape, len(shape) - 1)
    f = jnp.float32
    return (
        (lane % 16 != 0).astype(f),
        (lane % 16 != 15).astype(f),
        (lane >= 16).astype(f),
        (lane < 112).astype(f),
    )


def compute_kernel(n_own, plan, landed, finished, tiled, img, cot, kout, grad, xa, ra, ta, xb, rb, tb, *rest):
    ub, ua, save = rest[:6], rest[6:12], (rest[12:23], rest[23:34])
    f32 = jnp.float32
    unit_count, slot_count, unit_of, turned = plan()
    left, right, upper, lower = lane_masks((16, 128))

    row3 = lax.broadcasted_iota(jnp.int32, (BATCH, 8, 128), 1)
    masks3 = lane_masks((BATCH, 8, 128))

    def image_blur(v):
        even = row3 % 2 == 0
        mate = jnp.where(even, pltpu.roll(v, 7, 1), pltpu.roll(v, 1, 1))
        side = jnp.where(even, masks3[0] * pltpu.roll(mate, 1, 2), masks3[1] * pltpu.roll(mate, 127, 2))
        h = v + mate + side
        above = pltpu.roll(h, 2, 1)
        below = pltpu.roll(h, 6, 1)
        above = jnp.where(row3 < 2, masks3[2] * pltpu.roll(above, 16, 2), above)
        below = jnp.where(row3 >= 6, masks3[3] * pltpu.roll(below, 112, 2), below)
        return h + above + below

    def prologue(step, carry):
        at = pl.multiple_of(step * BATCH, BATCH)
        at8 = pl.ds(pl.multiple_of(step * BATCH * 8, BATCH * 8), BATCH * 8)
        val = img[pl.ds(at, BATCH)].astype(f32)
        var = jnp.zeros((BATCH, 8, 128), f32)
        for ch in range(3):
            x = val[:, ch * 8 : ch * 8 + 8, :]
            xa[ch, at8, :] = x.reshape(BATCH * 8, 128)
            var = var + x * x
        var = var * (1.0 / 3.0)
        for layer in range(LAYERS):
            area = (WEIGHT_VAR / 9.0) * image_blur(var) + BIAS_VAR
            inv = lax.rsqrt(area)
            ra[layer, at8, :] = (inv * math.sqrt(ALPHA[layer])).reshape(BATCH * 8, 128)
            ta[layer, at8, :] = (
                area * inv * (1.0 / math.sqrt(2.0 * math.pi * ALPHA[layer]))
            ).reshape(BATCH * 8, 128)
            var = 0.5 * area
        for k in range(6):
            ua[k][at8, :] = jnp.zeros((BATCH * 8, 128), f32)
        return carry

    more = slot_count > 34

    def fetched(step, carry):
        landed(step)
        return prologue(step, carry)

    lax.fori_loop(0, 4, fetched, 0)
    lax.fori_loop(8, jnp.where(more, TABLE // BATCH, 9), fetched, 0)
    fetched(4, 0)

    for group in range(n_own // 8):
        for s in range(8):
            rows = pl.ds(group * 64 + s, 8, stride=8)
            part = slice(group * 8, group * 8 + 8)
            for q in range(3):
                xb[q, s, part, :] = xa[q, rows, :]
                rb[q, s, part, :] = ra[q, rows, :]
                tb[q, s, part, :] = ta[q, rows, :]
    for k in range(6):
        ub[k][...] = jnp.zeros_like(ub[k])
    kout[...] = jnp.zeros_like(kout)

    def across(v):
        out = [None] * 8
        for p in range(0, 8, 2):
            mid = v[p] + v[p + 1]
            out[p] = mid + left * pltpu.roll(v[p + 1], 1, 1)
            out[p + 1] = mid + right * pltpu.roll(v[p], 127, 1)
        return out

    def vertical(h, bias):
        w = [None] * 8
        for sx in range(2):
            top = upper * pltpu.roll(h[6 + sx], 16, 1)
            bottom = lower * pltpu.roll(h[sx], 112, 1)
            one = h[sx] + h[2 + sx]
            two = h[4 + sx] + h[6 + sx]
            if bias is not None:
                one = one + bias
                two = two + bias
            w[sx] = one + top
            w[2 + sx] = one + h[4 + sx]
            w[4 + sx] = h[2 + sx] + two
            w[6 + sx] = two + bottom
        return w

    lane16 = lax.broadcasted_iota(jnp.int32, (16, 128), 1)
    row16 = lax.broadcasted_iota(jnp.int32, (16, 128), 0)
    ORDER = (0, 7, 1, 6, 2, 5, 3, 4)

    def ready(u):
        slot, bb, tile, lane = unit_of(u)
        base = pl.multiple_of((n_own + slot) * 8, 8)
        own = pl.ds(pl.multiple_of(bb * 16, 16), 16)
        return base, own, tile, lane

    def arow(ref, q, base, s):
        return ref[q, pl.ds(base + s, 1), :]

    def fold(uacc, k, base):
        total = uacc[k][pl.ds(0, 8, stride=8), :]
        for b in range(1, 8):
            total = total + uacc[k][pl.ds(b, 8, stride=8), :]
        ua[k][pl.ds(base, 8), :] += total

    def tally(uacc, k, s, own, e_own, e_slot):
        ub[k][s, own, :] += e_own
        uacc[k][s * 8 : s * 8 + 8, :] = e_slot[:8] + e_slot[8:]

    def forward(u, saved):
        sg1, sz1, sg2, sz2, sh, *uacc = saved
        base, own, tile, lane = ready(u)
        h = [None] * 8
        for s in ORDER:
            x = xb[0, s, own, :] * arow(xa, 0, base, s)
            x = x + xb[1, s, own, :] * arow(xa, 1, base, s)
            x = x + xb[2, s, own, :] * arow(xa, 2, base, s)
            h[s] = x
        h = across(h)
        spin = turned(u)
        row = cot[pl.ds(tile * 16 + lane, 1), :]
        source = jnp.where(spin, jnp.broadcast_to(row, (16, 128)), cot[pl.ds(pl.multiple_of(tile * 16, 16), 16), :])
        weight = jnp.where(lane16 == jnp.where(spin, row16, lane), source, 0.0)
        weight = jnp.sum(weight, axis=1, keepdims=True) * (WEIGHT_VAR * ALPHA[2] / 1024.0)
        weight = jnp.broadcast_to(weight, (16, 128))
        total = None
        for layer in range(LAYERS):
            w = vertical(h, BIAS[layer])
            h = [None] * 8
            for s in ORDER:
                c = (w[s] * rb[layer, s, own, :]) * arow(ra, layer, base, s)
                y = jnp.maximum(1.0 - c * c, TINY)
                sine = y * lax.rsqrt(y)
                v = lax.rsqrt(1.0 + sine)
                poly = ASIN[4] * v + ASIN[3]
                for k in range(2, -1, -1):
                    poly = poly * v + ASIN[k]
                g = c * poly + 0.25
                z = (sine * tb[layer, s, own, :]) * arow(ta, layer, base, s)
                f = w[s] * g + z
                if layer < LAYERS - 1:
                    (sg1, sg2)[layer][s] = g
                    (sz1, sz2)[layer][s] = z
                    h[s] = f
                else:
                    total = f if total is None else total + f
                    e = weight * z
                    tally(uacc, layer, s, own, e, e)
                    h[s] = weight * g
            h = across(h)
        for s in range(8):
            sh[s] = h[s]
        fold(uacc, LAYERS - 1, base)
        value = jnp.sum(total, axis=1, keepdims=True) * (WEIGHT_VAR * ALPHA[2] / 1024.0) + BIAS_VAR
        value = jnp.broadcast_to(value, (16, 128))
        flat = jnp.sum(jnp.where(lane16 == row16, value, 0.0), axis=0, keepdims=True)
        value = jnp.where(spin, jnp.broadcast_to(flat, (16, 128)), value)
        kout[tile] = jnp.where(jnp.where(spin, row16, lane16) == lane, value, kout[tile])

    def backward(u, saved):
        sg1, sz1, sg2, sz2, sh, *uacc = saved
        base, own, tile, lane = ready(u)
        h = [sh[s] for s in range(8)]
        for layer in range(LAYERS - 2, -1, -1):
            w = vertical(h, None)
            h = [None] * 8
            for s in ORDER:
                e = w[s] * (sz1, sz2)[layer][s]
                tally(uacc, layer, s, own, e, e)
                h[s] = w[s] * (sg1, sg2)[layer][s]
            h = across(h)
            fold(uacc, layer, base)
        w = vertical(h, None)
        for s in range(8):
            for q in range(3):
                tally(uacc, 3 + q, s, own, w[s] * arow(xa, q, base, s), w[s] * xb[q, s, own, :])
        for q in range(3):
            fold(uacc, 3 + q, base)

    forward(jnp.int32(0), save[0])
    forward(jnp.int32(1), save[1])

    def gather_own(block):
        for group in (2 * block, 2 * block + 1):
            for s in range(8):
                rows = pl.ds(group * 64 + s, 8, stride=8)
                for k in range(6):
                    ua[k][rows, :] = ub[k][s, group * 8 : group * 8 + 8, :]

    def pairs(j, carry):
        @pl.when(jnp.logical_or(j == 2, jnp.logical_or(j == 4, j == 6)))
        def _():
            fetched(4 + (j >> 1), 0)

        for n in range(2):
            u = 4 * j + 2 * n
            backward(u, save[0])
            forward(u + 2, save[0])
            backward(u + 1, save[1])
            forward(u + 3, save[1])

        @pl.when(jnp.logical_or(j == 4, jnp.logical_or(j == 10, jnp.logical_or(j == 12, j == 14))))
        def _():
            low = jnp.where(j == 4, 8, (j >> 1) - 1)
            high = jnp.where(jnp.logical_and(j == 4, more), TABLE // BATCH, low + 1)
            lax.fori_loop(low, high, last, 0)

        @pl.when(j == 12)
        def _():
            gather_own(0)
            lax.fori_loop(0, 2, last, 0)

        return carry

    def epilogue(step, carry):
        at = pl.multiple_of(step * BATCH, BATCH)
        at8 = pl.ds(pl.multiple_of(step * BATCH * 8, BATCH * 8), BATCH * 8)
        down = None
        for layer in range(LAYERS - 1, -1, -1):
            r = ra[layer, at8, :]
            d = ua[layer][at8, :] * (r * r) * (0.5 / ALPHA[layer])
            d = d.reshape(BATCH, 8, 128)
            if down is not None:
                d = d + 0.5 * down
            down = (WEIGHT_VAR / 9.0) * image_blur(d)
        down = down * (2.0 / 3.0)
        for q in range(3):
            x = xa[q, at8, :].reshape(BATCH, 8, 128)
            part = ua[3 + q][at8, :].reshape(BATCH, 8, 128)
            grad[pl.ds(at, BATCH), q * 8 : q * 8 + 8, :] = part + down * x
        return carry

    def last(step, carry):
        epilogue(step, 0)
        finished(step)
        return carry

    lax.fori_loop(0, (unit_count - 2) // 4, pairs, 0)
    tiled()
    backward(jnp.int32(unit_count - 2), save[0])
    backward(jnp.int32(unit_count - 1), save[1])
    gather_own(1)
    lax.fori_loop(2, 4, last, 0)
    last(7, 0)


def lane_order(flip):
    a = lax.broadcasted_iota(jnp.int32, (128, 128), 1 if flip else 0)
    b = lax.broadcasted_iota(jnp.int32, (128, 128), 0 if flip else 1)
    to = ((a >> 5) * 2 + (a & 1)) * 16 + ((a >> 1) & 15)
    return jnp.where(to == b, 1.0, 0.0)


def swap_groups(rows):
    group = lax.broadcasted_iota(jnp.int32, rows[0].shape, 1) >> 4
    out = []
    for s in range(8):
        total = rows[s]
        for j in range(8):
            if j != s:
                total = jnp.where(group == j, pltpu.roll(rows[j], (j - s) * 16 % 128, 1), total)
        out.append(total)
    return out


def to_rows(images, spread, mine):
    order = lane_order(False).astype(jnp.bfloat16)
    for ch in range(3):
        tall = jnp.concatenate(
            [images[:, (ch * 8 + j) * 128 : (ch * 8 + j + 1) * 128].astype(jnp.float32) for j in range(8)]
        )
        tall = jnp.dot(tall.astype(jnp.bfloat16), order, preferred_element_type=jnp.float32)
        rows = swap_groups([tall[4 * j : 4 * j + 4] for j in range(8)])
        for s in range(8):
            spread[pl.ds(ch * 8 + s, 4, stride=24), :] = rows[s]
    for k in range(4):
        mine[k] = spread[24 * k : 24 * k + 24, :].astype(jnp.bfloat16)


def from_rows(spread, out):
    order = lane_order(True)
    for ch in range(3):
        rows = swap_groups([spread[pl.ds(ch * 8 + s, 4, stride=24), :] for s in range(8)])
        tall = jnp.dot(
            jnp.concatenate(rows), order, precision=lax.Precision.HIGHEST, preferred_element_type=jnp.float32
        )
        for j in range(8):
            out[:, (ch * 8 + j) * 128 : (ch * 8 + j + 1) * 128] = tall[4 * j : 4 * j + 4]


ROWS = 16
COLS = 8
EXTRA = 18
SLOTS = 32 + EXTRA
TABLE = 88
TILES = 6
MESH = pl.DeviceIdType.MESH


def place():
    return lax.axis_index("row"), lax.axis_index("col")


def greet(r, c):
    barrier = pltpu.get_barrier_semaphore()

    def tell(go, rr, cc):
        away = jnp.logical_or(rr != r, cc != c)
        guarded(
            go, away, lambda: pl.semaphore_signal(barrier, inc=1, device_id=(rr, cc), device_id_type=MESH)
        )

    for slot in range(66):
        _, rr, cc, _, _ = partial_route(r, c, slot // BATCH, slot % BATCH)
        tell(None, rr, cc)
    rr, cc, _, _ = tile_route(r, c, 4)
    tell(None, rr, cc)

    @pl.when(c == 0)
    def _():
        for slot in range(66, 32 + SLOTS):
            _, rr, cc, _, _ = partial_route(r, c, slot // BATCH, slot % BATCH)
            tell(None, rr, cc)
        rr, cc, _, _ = tile_route(r, c, 5)
        tell(None, rr, cc)


def enter(r, c):
    count = jnp.int32(0)
    for _, _, _, _, away in image_routes(r, c):
        count += 1 if away is None else away.astype(jnp.int32)
    for k in range(4):
        dd, _, straight, _, _, _ = cot_route(r, c, 0, k)
        count += jnp.where(dd == 8, 7 + jnp.where(straight, 0, 1), 0)
        dd, _, straight, _, _, _ = cot_route(r, c, 1, k)
        here = jnp.logical_and(straight, c == 0)
        count += jnp.where(jnp.logical_and(dd == 8, jnp.logical_not(here)), 1, 0)
    pl.semaphore_wait(pltpu.get_barrier_semaphore(), count)


def ship(go, away, rr, cc, src, dst, send_sem, recv_sem):
    def remote():
        pltpu.make_async_remote_copy(src, dst, send_sem, recv_sem, device_id=(rr, cc), device_id_type=MESH).start()

    def local():
        pltpu.make_async_copy(src, dst, recv_sem).start()

    guarded(go, away, remote)
    if away is not None:
        guarded(go, jnp.logical_not(away), local)


def shipped(go, away, rr, cc, src, dst, send_sem, recv_sem):
    guarded(go, away, lambda: pltpu.make_async_copy(src, src, send_sem).wait())


def guarded(one, two, work):
    conds = [x for x in (one, two) if x is not None]
    if not conds:
        work()
        return
    cond = conds[0] if len(conds) == 1 else jnp.logical_and(*conds)

    @pl.when(cond)
    def _():
        work()


def arrived(dst, recv_sem):
    pltpu.make_async_copy(dst, dst, recv_sem).wait()


def image_routes(r, c):
    e = ((c & 1) << 4) + r
    early = e < 16
    for k in range(4):
        block = 4 * k + (c >> 1)
        for i in range(COLS):
            d = (c + i) & 7
            yield k, block, d, e, (block != r if i == 0 else None)
            rr = (block + 16 - d) & 15
            yield k, rr, d, 32 + e, (rr != r if i == 0 else None)
        rr = (block + 8) & 15
        d = jnp.where(early, e >> 1, 0)
        slot = jnp.where(early, 64 + (e & 1), 50 + e)
        yield k, rr, d, slot, jnp.logical_or(rr != r, d != c)


def slot_count_of(c):
    return jnp.where(c == 0, 32 + EXTRA, 34)


def cot_route(r, c, h, k):
    q = c & 1
    block = 4 * k + (c >> 1)
    dd = block - r
    straight = jnp.logical_or(dd < 8, jnp.logical_and(dd == 8, q == h))
    single = jnp.logical_and(dd >= 0, dd != 8)
    if h == 1:
        single = jnp.logical_and(single, jnp.logical_or(dd != 0, q == 1))
    near = dd < 8
    rr = jnp.where(near, r, block)
    cc = jnp.where(near, dd, 16 - dd) & 7
    slot = jnp.where(near, h * 2 + q, q * 2 + h)
    return dd, single, straight, rr, cc, slot


def tangents(op, r, c, cots, tiles, cot_send, cot_recv, far_send):
    for h in range(2):
        for k in range(4):
            idx = h * 4 + k
            dd, single, straight, rr, cc, slot = cot_route(r, c, h, k)
            src = cots.at[idx]
            op(single, dd != c, rr, cc, src, tiles.at[slot], cot_send.at[idx], cot_recv.at[slot])

            @pl.when(dd == 8)
            def _():
                row = jnp.where(straight, r, (r + 8) & 15)
                for i in range(COLS if h == 0 else 1):
                    d = (c + i) & 7 if h == 0 else 0
                    away = jnp.logical_not(straight) if i == 0 else None
                    if h == 1:
                        away = jnp.logical_or(away, c != 0)
                    op(None, away, row, d, src, tiles.at[4 + h], far_send.at[h * 8 + i], cot_recv.at[4 + h])


def partial_route(r, c, batch, n):
    slot = batch * BATCH + n
    main = batch < 8
    own = batch < 4
    x = slot - 64
    e = jnp.where(main, slot & 31, jnp.where(x < 2, 2 * c + x, 14 + x))
    block = jnp.where(own, r, jnp.where(main, r + c, r + 8) & 15)
    j = 2 * block + (e >> 4)
    source = jnp.where(own, c, jnp.where(main, 8 + c, 16))
    return slot, e & 15, j & 7, j >> 3, source


def tile_route(r, c, slot):
    far = slot >= 4
    bb, qa = slot // 2, slot % 2
    other = (r + 8) & 15 if far else (r + c) & 15
    if far:
        bb = jnp.where(r < 8, qa, 1 - qa)
    ahead = other >= r
    i = jnp.where(ahead, 2 * r + bb, 2 * other + qa)
    j = jnp.where(ahead, 2 * other + qa, 2 * r + bb)
    return i >> 1, j & 7, i & 1, j >> 3


def whole_kernel(images_in, cot_in, images_out, kernel_ref, mine, cots, spread, cot32, kernel_out, *rest):
    table, tiles, grads, kouts, parts, far = rest[:6]
    img_send, img_recv, cot_send, cot_recv, far_send = rest[6:11]
    part_send, part_recv, tile_send, tile_recv, far_recv = rest[11:16]
    r, c = place()
    greet(r, c)
    to_rows(images_in, spread, mine)
    cot32[...] = jnp.zeros_like(cot32)
    for h in range(2):
        for row in range(16):
            part = cot_in[h, row].astype(jnp.float32)
            cot32[pl.ds(h * 64 + row, 4, stride=16), 0:16] = part
    for idx in range(8):
        cots[idx] = cot32[16 * idx : 16 * idx + 16, :].astype(jnp.bfloat16)
    enter(r, c)

    def images(op):
        for idx, (k, rr, cc, slot, away) in enumerate(image_routes(r, c)):
            op(None, away, rr, cc, mine.at[k], table.at[slot], img_send.at[idx], img_recv.at[slot])

    images(ship)
    tangents(ship, r, c, cots, tiles, cot_send, cot_recv, far_send)
    for slot in (0, 1, 3, 4):
        arrived(tiles.at[slot], cot_recv.at[slot])

    @pl.when(c != 0)
    def _():
        arrived(tiles.at[2], cot_recv.at[2])
        tiles[5] = jnp.zeros((16, 128), jnp.bfloat16)
        for slot in range(66, 72):
            table[slot] = jnp.zeros((24, 128), jnp.bfloat16)

    @pl.when(c == 0)
    def _():
        arrived(tiles.at[5], cot_recv.at[5])
        tiles[2] = jnp.zeros((16, 128), jnp.bfloat16)
        for slot in range(32 + SLOTS, TABLE):
            table[slot] = jnp.zeros((24, 128), jnp.bfloat16)

    def used(batch, n):
        slot = batch * BATCH + n
        return jnp.logical_or(slot < 66, jnp.logical_and(c == 0, slot < 32 + SLOTS))

    def landed(batch):
        for n in range(BATCH):
            slot = batch * BATCH + n
            guarded(used(batch, n), None, lambda: arrived(table.at[slot], img_recv.at[slot]))

    def partials(op, batch):
        for n in range(BATCH):
            slot, rr, cc, k, source = partial_route(r, c, batch, n)
            away = jnp.logical_or(rr != r, cc != c)
            op(used(batch, n), away, rr, cc, grads.at[slot], parts.at[k, source], part_send.at[slot], part_recv.at[k, source])

    def outputs(op):
        for slot in range(TILES):
            rr, cc, h, k = tile_route(r, c, slot)
            go = (None, None, c != 0, None, None, c == 0)[slot]
            if slot == 4:
                dst, sem = far.at[c], far_recv.at[c]
            else:
                dst, sem = kernel_out.at[pl.ds(pl.multiple_of((h * 4 + k) * 16, 16), 16)], tile_recv.at[h * 4 + k]
            away = jnp.logical_or(rr != r, cc != c)
            op(go, away, rr, cc, kouts.at[slot], dst, tile_send.at[slot], sem)

    for slot in range(TILES):
        cot32[16 * slot : 16 * slot + 16, :] = tiles[slot].astype(jnp.float32)

    compute_kernel(
        32, plan, landed, lambda batch: partials(ship, batch), lambda: outputs(ship), table, cot32, kouts, grads, *rest[16:]
    )


    for h in range(2):
        for k in range(4):
            dd, single, straight, rr, cc, slot = cot_route(r, c, h, k)
            spot = h * 4 + k
            if h == 0:

                @pl.when(dd == 8)
                def _():
                    for d in range(COLS):
                        arrived(far.at[d], far_recv.at[d])
                    total = far[0]
                    for d in range(1, COLS):
                        total = total + far[d]
                    kernel_out[16 * spot : 16 * spot + 16, :] = total

                get = single
            else:
                get = jnp.logical_or(single, dd == 8)

            @pl.when(get)
            def _():
                arrived(kernel_out.at[16 * spot : 16 * spot + 16], tile_recv.at[spot])

            unused = dd < 0
            if h == 1:
                unused = jnp.logical_or(unused, jnp.logical_and(dd == 0, (c & 1) == 0))

            @pl.when(unused)
            def _():
                kernel_out[16 * spot : 16 * spot + 16, :] = jnp.zeros((16, 128), jnp.float32)

    for k in range(4):
        for source in range(17):
            arrived(parts.at[k, source], part_recv.at[k, source])
        total = parts[k, 0]
        for source in range(1, 17):
            total = total + parts[k, source]
        spread[24 * k : 24 * k + 24, :] = total

    from_rows(spread, images_out)
    for h in range(2):
        for row in range(16):
            kernel_ref[h, row] = kernel_out[pl.ds(h * 64 + row, 4, stride=16), :][:, 0:16]
    images(shipped)
    tangents(shipped, r, c, cots, tiles, cot_send, cot_recv, far_send)
    outputs(shipped)

    def settle(batch, carry):
        partials(shipped, batch)
        return carry

    lax.fori_loop(0, TABLE // BATCH, settle, 0)


def whole_call(mine, cots):
    whole = pl.BlockSpec(memory_space=pltpu.VMEM)
    dma = pltpu.SemaphoreType.DMA
    vm = lambda *shape: pltpu.VMEM(shape, jnp.float32)
    own, rows = 32, TABLE * 8
    return pl.pallas_call(
        whole_kernel,
        out_shape=(
            jax.ShapeDtypeStruct((4, 3072), jnp.float32),
            jax.ShapeDtypeStruct((2, 16, 4, 16), jnp.float32),
        ),
        in_specs=[whole, whole],
        out_specs=(whole, whole),
        scratch_shapes=[
            pltpu.VMEM((4, 24, 128), jnp.bfloat16),
            pltpu.VMEM((8, 16, 128), jnp.bfloat16),
            vm(96, 128),
            vm(128, 128),
            vm(128, 128),
            pltpu.VMEM((TABLE, 24, 128), jnp.bfloat16),
            pltpu.VMEM((TILES, 16, 128), jnp.bfloat16),
            vm(TABLE, 24, 128),
            vm(TILES, 16, 128),
            vm(4, 17, 24, 128),
            vm(8, 16, 128),
        ]
        + [dma((68,)), dma((32 + SLOTS,)), dma((8,)), dma((TILES,)), dma((16,))]
        + [dma((32 + SLOTS,)), dma((4, 17)), dma((TILES,)), dma((8,)), dma((8,))]
        + [vm(3, rows, 128)] * 3
        + [vm(3, 8, own, 128)] * 3
        + [vm(8, own, 128)] * 6
        + [vm(rows, 128)] * 6
        + ([vm(8, 16, 128)] * 5 + [vm(64, 128)] * 6) * 2,
        compiler_params=pltpu.CompilerParams(
            collective_id=0, has_side_effects=True, vmem_limit_bytes=56 * 1024 * 1024
        ),
    )(mine, cots)


def plan():
    r, c = place()

    first = c == 0
    extras = jnp.where(first, EXTRA, 2)

    def unit_of(u):
        v = u - extras
        main = v >= 0
        e = jnp.where(u < 2, 2 * c + u, 14 + u)
        half = jnp.where(r < 8, e >> 4, 1 - (e >> 4))
        early = v < 32
        slot = jnp.where(main, jnp.where(early, v, v - jnp.where(first, 16, 32)), 32 + u)
        bb = jnp.where(main, jnp.where(early, 0, 1), half)
        tile = jnp.where(main, bb * 2 + (slot >> 4), 4 + (e >> 4))
        return slot, bb, tile, jnp.where(main, slot, e) & 15

    def turned(u):
        return jnp.where(u < extras, r >= 8, r + c >= ROWS)

    return 66, slot_count_of(c), unit_of, turned


def body(images, cotangent):
    image_grads, kernel = whole_call(images.reshape(4, 3072), cotangent.reshape(2, 16, 4, 16))
    return kernel.reshape(2, 16, 4, 1, 16), image_grads.reshape(4, 1, 1, 3072)


def solution(mesh):
    return jax.shard_map(
        body,
        mesh=mesh,
        in_specs=(P(None, "col", "row", None), P("row", None, None, "col", None)),
        out_specs=(P("row", None, None, "col", None), P(None, "col", "row", None)),
        check_vma=False,
    )
```
